32 devices in a mesh: gx: 8 (over y, x, core), gy: 4 (over z).
Axes of the slice: x: 2, y: 2, z: 4, core: 2. Of those that a mesh axis runs over, the one named last changes fastest.
Arguments:
- velocity: float32 [3, 32, 256, 2048], P(None, None, 'gx', 'gy'), may hold values from -6 to 6
- fiber_points: float32 [256, 3, 128], P(('gx', 'gy')), may hold values from -6 to 6
- stiffness: float32 [256], P(('gx', 'gy')), may hold values from 0.5 to 2
- links: int32 [256, 128], P(('gx', 'gy')), may hold values from 1 to 127
- delta_weights: bfloat16 [256, 8, 128, 512], P(('gx', 'gy')), may hold values from -0.5 to 0.5
- owners: int32 [256, 8, 1], P(('gx', 'gy')), may hold values from 0 to 31; in each aligned block of 64 rows (0 to 63, 64 to 127, ..., all dimensions but the last counted through in order) at most 4 rows name the same one
- patch_slots: int32 [256, 8], P(('gx', 'gy')), may hold values from 0 to 1023
Outputs:
- fluid: float32 [3, 32, 256, 2048], P(None, None, 'gx', 'gy')
- moved_points: float32 [256, 3, 128], P(('gx', 'gy'))
The draws below stay inside these ranges and needn't reach their ends.
Inputs may be any that keep to these rules, and one draw needn't show every extreme that they name: owners counts devices in the order gx slower, gy faster; among the rows of one device, no owner is named more than 4 times, a bound that some block reaches.
All inputs are finite; a program needn't handle non-finite values.
Results may differ from the reference program's by a relative error of at most 0.0037.
Values may be sent and summed in bfloat16 or wider, within the bound.
A program may use at most 128 MiB of HBM per device.

```python
import math
import jax
import jax.numpy as jnp
import numpy as np
from jax import lax

CX = 32
CY = 512
NZ = 32
PATCH = 512
FBP = 128
FBD = 8
INTERSECTION = 8
STEPS = 2
NX = 256
NY = 2048
CAP = 4
P_DEV = 1024
FIBERS_B = 256
N_GX = 8
N_GY = 4
DEVICES = 32


def set_ends(drawn, own_key, smallest, high):
    longest = drawn.shape.index(max(drawn.shape))
    spots = []
    for shift in (0, 1):
        where = [jax.random.randint(jax.random.fold_in(own_key, axis), (), 0, length) for axis, length in enumerate(drawn.shape)]
        where[longest] = (where[longest] + shift) % drawn.shape[longest]
        spots.append(tuple(where))
    return drawn.at[spots[0]].set(smallest).at[spots[1]].set(high)


def steps_of(own_key, shape, split, least, largest):
    gain, own = 1.0, jax.random.fold_in(own_key, 6)
    for axis_at, blocks in split:
        draws = jnp.exp(jax.random.uniform(jax.random.fold_in(own, axis_at), (blocks,), jnp.float32, least / len(split), largest / len(split)))
        gain = gain * jnp.repeat(draws, shape[axis_at] // blocks).reshape([-1 if axis == axis_at else 1 for axis in range(len(shape))])
    return gain


def deal_out(key, own, number, rows, amount, top, most, slope):
    order = jax.random.permutation(key, amount)
    crowded, common = load_shares(amount, rows * top, most, slope, True), load_shares(amount, rows * top, most, slope, False)
    places = jnp.arange(amount)

    def named(lengths, turn):
        used = int((lengths > 0).sum())
        fixed = max(1, used // 4)
        passed = fixed + (places - fixed + turn * (used - fixed)) % max(1, amount - fixed)
        return jnp.zeros((amount,), jnp.int32).at[order[jnp.where(places < fixed, places, passed)]].set(jnp.asarray(lengths, jnp.int32))

    lengths = jnp.where(number % 4 == 0, named(crowded, number // 4), named(common, number - number // 4 - 1))
    mixed = jax.random.permutation(jax.random.fold_in(own, 3), amount)
    donor, taker = mixed[0:amount // 2 * 2:2], mixed[1:amount // 2 * 2:2]
    margin = jnp.minimum(lengths[donor] - 1, most - lengths[taker]) // 2
    margin = jnp.where((donor == order[0]) | (taker == order[0]) | (lengths[taker] == 0), 0, jnp.maximum(margin, 0))
    passed = jax.random.randint(jax.random.fold_in(own, 4), (amount // 2,), 0, 1 << 20) % (margin + 1)
    lengths = lengths.at[donor].add(-passed).at[taker].add(passed)
    labels = jnp.searchsorted(jnp.cumsum(lengths), jnp.arange(rows * top), side="right").astype(jnp.int32)
    grid = labels.reshape(top, rows).T
    grid = grid[jax.random.permutation(jax.random.fold_in(own, 1), rows)]
    turn = jax.random.randint(jax.random.fold_in(own, 2), (rows, 1), 0, top)
    return jnp.take_along_axis(grid, (jnp.arange(top)[None, :] + turn) % top, axis=1)


def load_shares(amount, total, limit, slope, full):
    portions = [(1 << 20) // math.isqrt(rank ** slope) + 1 for rank in range(1, amount + 1)]
    largest = limit if full else min(limit, max(-(-total // amount), total * portions[0] // sum(portions)))
    least = 1 if total - largest >= amount - 1 else 0
    given, surplus = [largest] + [least] * (amount - 1), total - largest - least * (amount - 1)
    while surplus > 0:
        candidates = [i for i in range(1, amount) if given[i] < largest] or [i for i in range(1, amount) if given[i] < limit]
        mass, left = sum([portions[i] for i in candidates]), surplus
        for i in candidates:
            more = min(limit - given[i], max(1, left * portions[i] // mass), surplus)
            given[i] = given[i] + more
            surplus = surplus - more
    return np.array(given)


def bell_draw(stream_key, dims, deviation, bound, shards=(), kind=jnp.bfloat16):
    entries = jax.random.normal(stream_key, dims, jnp.float32) * deviation
    if len(shards) > 0:
        entries = steps_of(stream_key, dims, shards, -0.22, 0.18) * entries
    return jnp.clip(entries, min=-bound, max=bound).astype(kind)


def setup_inputs(seed: int = 0) -> dict:
    seeds = jax.random.split(jax.random.key(seed), 8)
    velocity = bell_draw(seeds[0], (3, NZ, NX, NY), 1.0, 6.0, ((2, 8), (3, 4)), jnp.float32)
    fiber_points = bell_draw(seeds[1], (FIBERS_B, 3, FBP), 1.0, 6.0, ((0, 32),), jnp.float32)
    stiffness = jnp.clip(jnp.exp(math.log(2.0) - 1.3862944 * jax.random.uniform(seeds[2], (FIBERS_B,), jnp.float32) ** steps_of(seeds[2], (FIBERS_B,), ((0, 32),), -0.2, 0.2)), 0.5, 2.0)
    links = set_ends(jax.random.randint(seeds[3], (FIBERS_B, FBP), 1, FBP), jax.random.fold_in(seeds[3], 1), 1, FBP - 1).astype(jnp.int32)
    delta_weights = bell_draw(seeds[4], (FIBERS_B, INTERSECTION, FBP, PATCH), FBP ** -0.5, 0.5, ((0, 32),))
    owners_keys = jax.random.split(jax.random.fold_in(seeds[5], 1), FIBERS_B * INTERSECTION // (FBD * INTERSECTION))
    owners_turns = jax.random.permutation(jax.random.fold_in(seeds[5], 3), FIBERS_B * INTERSECTION // (FBD * INTERSECTION))
    owners = jax.vmap(lambda own, number: deal_out(jax.random.fold_in(seeds[5], 2), own, number, FBD * INTERSECTION, DEVICES, 1, CAP, 2))(owners_keys, owners_turns).reshape((FIBERS_B, INTERSECTION, 1))
    patch_slots = set_ends(jax.random.randint(seeds[6], (FIBERS_B, INTERSECTION), 0, P_DEV), jax.random.fold_in(seeds[6], 1), 0, P_DEV - 1).astype(jnp.int32)
    return dict(velocity=velocity, fiber_points=fiber_points, stiffness=stiffness, links=links, delta_weights=delta_weights, owners=owners, patch_slots=patch_slots)


viscosity = 0.1
transport_rate = 0.1
force_step = 0.5
fiber_step = 0.25


def advance(extended):
    middle = extended[:, :, 1:-1, 1:-1]
    east_cells = extended[:, :, 2:, 1:-1]
    west_cells = extended[:, :, :-2, 1:-1]
    north_cells = extended[:, :, 1:-1, 2:]
    south_cells = extended[:, :, 1:-1, :-2]
    above_cells = jnp.roll(middle, -1, axis=1)
    below_cells = jnp.roll(middle, 1, axis=1)
    laplace = east_cells + west_cells + north_cells + south_cells + above_cells + below_cells - 6.0 * middle
    transport = middle[0:1] * (east_cells - west_cells) + middle[1:2] * (north_cells - south_cells) + middle[2:3] * (above_cells - below_cells)
    return middle + viscosity * laplace - transport_rate * transport


def reference(velocity, fiber_points, stiffness, links, delta_weights, owners, patch_slots):
    device_count = N_GX * N_GY
    patch_count = CX * CY * NZ // PATCH
    partner = (jnp.arange(FBP, dtype=jnp.int32)[None, :] + links) % FBP
    partner_full = jnp.broadcast_to(partner[:, None, :], fiber_points.shape)
    partner_points = jnp.take_along_axis(fiber_points, partner_full, axis=2)
    fiber_force = stiffness[:, None, None] * (partner_points - fiber_points)
    force_bf = fiber_force.astype(jnp.bfloat16)
    contrib = jnp.einsum("bcp,bkpq->bkcq", force_bf.astype(jnp.float32), delta_weights.astype(jnp.float32), precision=lax.Precision.HIGHEST)
    target = (owners[:, :, 0] * patch_count + patch_slots).reshape(-1).astype(jnp.int32)
    patches = jnp.zeros((device_count * patch_count, 3, PATCH), jnp.float32)
    patches = patches.at[target].add(contrib.reshape(-1, 3, PATCH))
    field = patches.reshape(N_GX, N_GY, patch_count, 3, PATCH).transpose(3, 0, 1, 2, 4)
    field = field.reshape(3, N_GX, N_GY, NZ, CX, CY).transpose(0, 3, 1, 4, 2, 5).reshape(3, NZ, NX, NY)
    moving = velocity + force_step * field
    for step_index in range(STEPS):
        moving = advance(jnp.pad(moving, ((0, 0), (0, 0), (1, 1), (1, 1))))
    fluid_bf = moving.astype(jnp.bfloat16)
    patch_view = fluid_bf.reshape(3, NZ, N_GX, CX, N_GY, CY).transpose(2, 4, 0, 1, 3, 5)
    patch_view = patch_view.reshape(device_count, 3, patch_count, PATCH).transpose(0, 2, 1, 3)
    patch_view = patch_view.reshape(device_count * patch_count, 3, PATCH)
    picked = patch_view[target].reshape(FIBERS_B, INTERSECTION, 3, PATCH)
    interp = jnp.einsum("bkcq,bkpq->bcp", picked.astype(jnp.float32), delta_weights.astype(jnp.float32), precision=lax.Precision.HIGHEST)
    return moving, fiber_points + fiber_step * interp
```

```python
import functools

import jax
import jax.numpy as jnp
from jax import lax
from jax.experimental import pallas as pl
from jax.experimental.pallas import tpu as pltpu
from jax.sharding import PartitionSpec as P

STEPS = 2
viscosity = 0.1
transport_rate = 0.1
force_step = 0.5
fiber_step = 0.25

F32 = jnp.float32
BF16 = jnp.bfloat16
I32 = jnp.int32
LANES = 128
MESH = pl.DeviceIdType.MESH
VMEM = pl.BlockSpec(memory_space=pltpu.VMEM)
ANY = pl.BlockSpec(memory_space=pl.ANY)
SMEM = pl.BlockSpec(memory_space=pltpu.SMEM)


def iota(shape, dim):
    return lax.broadcasted_iota(I32, shape, dim)


def to_column(row):
    n = row.shape[1]
    return jnp.sum(jnp.where(iota((n, n), 0) == iota((n, n), 1), row, 0), axis=1, keepdims=True)


def slot_row(owner_row, owner_column, devices):
    n = owner_row.shape[1]
    same = (owner_column == owner_row) & (iota((n, n), 0) < iota((n, n), 1))
    rank = jnp.sum(jnp.where(same, 1, 0), axis=0, keepdims=True)
    return rank * devices + owner_row


def slot_column(owner_row, owner_column, devices):
    n = owner_row.shape[1]
    same = (owner_column == owner_row) & (iota((n, n), 1) < iota((n, n), 0))
    rank = jnp.sum(jnp.where(same, 1, 0), axis=1, keepdims=True)
    return rank * devices + owner_column


def spread_kernel(
    devices, per_owner, points_ref, stiffness_ref, links_ref, owners_ref, slots_ref, weights_ref,
    out_ref, table_ref, force_ref, contrib_ref, stage_ref,
):
    b = pl.program_id(0)
    blocks = pl.num_programs(0)
    k, points, patch = weights_ref.shape[1:]

    @pl.when(b == 0)
    def _():
        partner = lax.rem(iota(links_ref.shape, 1) + links_ref[...], points)
        for c in range(3):
            here = points_ref[:, c, :]
            there = jnp.take_along_axis(here, partner, axis=1)
            force_ref[c] = stiffness_ref[...] * (there - here)

    diagonal = iota((k, k * points), 0) == iota((k, k * points), 1) // points
    rows = []
    for c in range(3):
        row = force_ref[c, pl.ds(b, 1), :]
        rows.append(jnp.where(diagonal, jnp.concatenate([row] * k, axis=1), 0.0))
    rows.append(jnp.zeros_like(rows[0]))
    left = jnp.concatenate(rows, axis=0).astype(BF16)
    right = weights_ref[0].reshape(k * points, patch)
    result = jnp.dot(left, right, preferred_element_type=F32)
    for c in range(3):
        contrib_ref[c, pl.ds(pl.multiple_of(b * k, k), k), :] = result[c * k:(c + 1) * k]

    @pl.when(b == blocks - 1)
    def _():
        owner_row = owners_ref[...]
        owner_column = to_column(owner_row)
        places = slot_row(owner_row, owner_column, devices)
        total = devices * per_owner
        chosen = iota((total, places.shape[1]), 0) == places
        selector = chosen.astype(F32).astype(BF16)
        tiles = patch // LANES
        width = 3 * tiles * per_owner
        for c in range(3):
            packed = jnp.dot(selector, contrib_ref[c].astype(BF16), preferred_element_type=F32)
            for p in range(per_owner):
                for t in range(tiles):
                    stage_ref[pl.ds(p * 3 * tiles + c * tiles + t, devices, stride=width), :] = (
                        packed[p * devices:(p + 1) * devices, t * LANES:(t + 1) * LANES]
                    )
        out_ref[...] = stage_ref[...].reshape(out_ref.shape).astype(BF16)
        column = jnp.max(jnp.where(chosen, slots_ref[...], -1), axis=1, keepdims=True)
        lane = iota((devices, LANES), 1)
        table = jnp.full((devices, LANES), -1, I32)
        for p in range(per_owner):
            table = jnp.where(lane == p, column[p * devices:(p + 1) * devices], table)
        for d in range(devices):
            table_ref[d] = table[d:d + 1]


def greet(others):
    barrier = pltpu.get_barrier_semaphore()
    for other in others:
        pl.semaphore_signal(barrier, inc=1, device_id=other, device_id_type=MESH)
    pl.semaphore_wait(barrier, len(others))


def swap_kernel(rows, columns, count, *refs):
    ins, outs = refs[:count], refs[count:2 * count]
    send_sem, recv_sem, own_sem = refs[2 * count:]
    devices = rows * columns
    me = lax.axis_index("gx") * columns + lax.axis_index("gy")

    def place(d):
        return (d // columns, lax.rem(d, columns))

    barrier = pltpu.get_barrier_semaphore()

    def hello(off, carry):
        other = lax.rem(me + off, devices)
        pl.semaphore_signal(barrier, inc=1, device_id=place(other), device_id_type=MESH)
        return carry

    lax.fori_loop(1, devices, hello, 0)
    pl.semaphore_wait(barrier, devices - 1)

    def copy(n, off):
        other = lax.rem(me + off, devices)
        return pltpu.make_async_remote_copy(
            src_ref=ins[n].at[other], dst_ref=outs[n].at[me],
            send_sem=send_sem.at[n, off], recv_sem=recv_sem.at[n, off],
            device_id=place(other), device_id_type=MESH,
        )

    def start(off, carry):
        for n in range(count):
            copy(n, off).start()
        return carry

    def finish(off, carry):
        for n in range(count):
            copy(n, off).wait()
        return carry

    lax.fori_loop(1, devices, start, 0)
    for n in range(count):
        pltpu.make_async_copy(ins[n].at[me], outs[n].at[me], own_sem.at[n]).start()
    for n in range(count):
        pltpu.make_async_copy(ins[n].at[me], outs[n].at[me], own_sem.at[n]).wait()
    lax.fori_loop(1, devices, finish, 0)


def swap(arrays, rows, columns, collective_id):
    devices = rows * columns
    count = len(arrays)
    return pl.pallas_call(
        functools.partial(swap_kernel, rows, columns, count),
        out_shape=[jax.ShapeDtypeStruct(a.shape, a.dtype) for a in arrays],
        in_specs=[VMEM] * count,
        out_specs=[VMEM] * count,
        scratch_shapes=[
            pltpu.SemaphoreType.DMA((count, devices)),
            pltpu.SemaphoreType.DMA((count, devices)),
            pltpu.SemaphoreType.DMA((count,)),
        ],
        compiler_params=pltpu.CompilerParams(collective_id=collective_id, has_side_effects=True),
    )(*arrays)


def unpack(stage_ref, devices, per_owner, tiles, c):
    width = 3 * tiles * per_owner
    rows = []
    for p in range(per_owner):
        rows.append(jnp.concatenate(
            [stage_ref[pl.ds(p * 3 * tiles + c * tiles + t, devices, stride=width), :]
             for t in range(tiles)], axis=1))
    return jnp.concatenate(rows, axis=0)


def add_kernel(
    devices, per_owner, received_ref, table_ref, velocity_ref,
    u_ref, sides_ref, ends_ref, corners_ref, stage_ref, force_ref, side_ref, corner_ref,
):
    i = pl.program_id(0)
    steps = pl.num_programs(0)
    _, depth, rows, columns = velocity_ref.shape
    tiles = columns // LANES
    total = devices * per_owner
    layers = depth * steps
    cells = depth * rows

    @pl.when(i == 0)
    def _():
        stage_ref[...] = received_ref[...].astype(F32).reshape(stage_ref.shape)
        for c in range(3):
            force_ref[c] = unpack(stage_ref, devices, per_owner, tiles, c).astype(BF16)
        corner_ref[...] = jnp.zeros_like(corner_ref)

    row = jnp.zeros((1, total), I32)
    for p in range(per_owner):
        column = table_ref[:, 0, :][:, p:p + 1]
        spot = iota((devices, total), 1) == p * devices + iota((devices, total), 0)
        row = row + jnp.sum(jnp.where(spot, column, 0), axis=0, keepdims=True)
    placing = (iota((cells, total), 0) + i * cells == row).astype(F32).astype(BF16)
    r16, c16 = iota((16, columns), 0), iota((16, columns), 1)
    pick = (r16 < 2) & (c16 == r16) | (r16 >= 2) & (r16 < 4) & (c16 == columns - 4 + r16)
    pick = pick.astype(F32).astype(BF16)
    cell, want = iota((cells, LANES), 0), iota((cells, LANES), 1)
    z, x = cell // rows + i * depth, lax.rem(cell, rows)
    edge = (x == 0) & (want == z) | (x == rows - 1) & (want == layers + z)
    edge = edge.astype(F32).astype(BF16)
    for c in range(3):
        push = jnp.dot(placing, force_ref[c], preferred_element_type=F32)
        u = velocity_ref[c] + force_step * push.reshape(depth, rows, columns)
        u_ref[c] = u
        for side in range(2):
            for r in range(2):
                x = r + side * (rows - 2)
                side_ref[side, c, r, pl.ds(pl.multiple_of(i * depth, depth), depth), :] = u_ref[c, :, x, :]
        flat = u.reshape(cells, columns).astype(BF16)
        ends = lax.dot_general(
            pick, flat, (((1,), (1,)), ((), ())), preferred_element_type=F32).astype(BF16)
        ends_ref[c] = ends
        corner_ref[c] += jnp.dot(ends, edge, preferred_element_type=F32)

    @pl.when(i == steps - 1)
    def _():
        sides_ref[...] = side_ref[...].astype(BF16)
        corners_ref[...] = corner_ref[...].astype(BF16)


def halo_kernel(
    rows, columns, sides_ref, ends_ref, corners_ref,
    sides_out, ends_out, corners_out, send_sem, recv_sem,
):
    gx, gy = lax.axis_index("gx"), lax.axis_index("gy")
    east, west = lax.rem(gx + 1, rows), lax.rem(gx + rows - 1, rows)
    north, south = lax.rem(gy + 1, columns), lax.rem(gy + columns - 1, columns)
    others = [
        (west, gy), (east, gy), (gx, south), (gx, north),
        (west, south), (west, north), (east, south), (east, north),
    ]
    greet(others)
    pairs = [
        (sides_ref.at[0], sides_out.at[1]), (sides_ref.at[1], sides_out.at[0]),
        (ends_ref, ends_out.at[1]), (ends_ref, ends_out.at[0]),
        (corners_ref, corners_out.at[3]), (corners_ref, corners_out.at[2]),
        (corners_ref, corners_out.at[1]), (corners_ref, corners_out.at[0]),
    ]
    copies = [
        pltpu.make_async_remote_copy(
            src_ref=source, dst_ref=target, send_sem=send_sem.at[n], recv_sem=recv_sem.at[n],
            device_id=other, device_id_type=MESH)
        for n, ((source, target), other) in enumerate(zip(pairs, others))
    ]
    for copy in copies:
        copy.start()
    for copy in copies:
        copy.wait()


def sweep(mid, east, west, north, south, above, below):
    r = transport_rate
    coefficients = [(viscosity - r * m, viscosity + r * m) for m in mid]
    keep = 1.0 - 6.0 * viscosity
    out = []
    for c in range(3):
        v = keep * mid[c]
        for (ahead, behind), (front, back) in zip(
            coefficients, ((east, west), (north, south), (above, below))
        ):
            v = v + (ahead * front[c] + behind * back[c])
        out.append(v)
    return out


def sweeps_kernel(
    devices, per_owner, chunk, flags_ref, sides_ref, ends_ref, corners_ref, table_ref, u_ref,
    fluid_ref, replies_ref, first_ref, second_ref, last_ref, side_ref, stage_ref, sum_ref,
    in_sem, out_sem,
):
    _, layers, rows, columns = u_ref.shape
    tiles = columns // LANES
    total = devices * per_owner
    chunks = layers // chunk

    def load(n):
        span = pl.ds(n * chunk, chunk)
        return pltpu.make_async_copy(
            u_ref.at[:, span], first_ref.at[:, span, 0:rows, 0:columns], in_sem.at[n])

    for n in range(chunks):
        load(n).start()

    has = [flags_ref[n] > 0 for n in range(4)]
    for side in range(2):
        side_ref[side, :, :, :, 0:columns] = jnp.where(has[side], sides_ref[side].astype(F32), 0.0)
        side_ref[side, :, :, :, columns:] = jnp.zeros((3, 2, layers, LANES), F32)
    r16, l16 = iota((16, LANES), 0), iota((16, LANES), 1)
    zero = jnp.zeros((16, LANES), F32)
    from_south = (r16 >= 2) & (r16 < 4) & (l16 == LANES - 4 + r16)
    from_north = (r16 < 2) & (l16 == r16)
    south_pick = jnp.where(has[2], from_south.astype(F32), zero).astype(BF16)
    north_pick = jnp.where(has[3], from_north.astype(F32), zero).astype(BF16)

    def expand(values, pick):
        return lax.dot_general(
            values, pick, (((0,), (0,)), ((), ())), preferred_element_type=F32)

    for c in range(3):
        band = expand(ends_ref[0, c], south_pick) + expand(ends_ref[1, c], north_pick)
        first_ref[c, :, 0:rows, columns:] = band.reshape(layers, rows, LANES)
        low = expand(corners_ref[0, c], south_pick) + expand(corners_ref[1, c], north_pick)
        high = expand(corners_ref[2, c], south_pick) + expand(corners_ref[3, c], north_pick)
        side_ref[0, c, 1, :, columns:] = jnp.where(has[0], low[layers:2 * layers], 0.0)
        side_ref[1, c, 0, :, columns:] = jnp.where(has[1], high[0:layers], 0.0)

    r8 = iota((8, columns + LANES), 0)

    def border(z, carry):
        for c in range(3):
            tile = jnp.zeros((8, columns + LANES), F32)
            for place, side, r in ((0, 1, 0), (1, 1, 1), (6, 0, 0), (7, 0, 1)):
                tile = jnp.where(r8 == place, side_ref[side, c, r, pl.ds(z, 1), :], tile)
            first_ref[c, pl.ds(z, 1), rows:, :] = tile[None]
        return carry

    lax.fori_loop(0, layers, border, 0)
    for n in range(chunks):
        load(n).wait()

    tall, wide = rows + 8, columns + LANES
    row, lane = iota((tall, wide), 0), iota((tall, wide), 1)
    keep = (
        (row < rows) | ((row == rows) & has[1]) | ((row == tall - 1) & has[0])
    ) & ((lane < columns) | ((lane == columns) & has[3]) | ((lane == wide - 1) & has[2]))

    def plane(ref, z):
        return [ref[c, z] for c in range(3)]

    def step_one(z, carry):
        up, down = lax.rem(z + 1, layers), lax.rem(z + layers - 1, layers)
        mid = plane(first_ref, z)
        east = [pltpu.roll(m, tall - 1, 0) for m in mid]
        west = [pltpu.roll(m, 1, 0) for m in mid]
        north = [pltpu.roll(m, wide - 1, 1) for m in mid]
        south = [pltpu.roll(m, 1, 1) for m in mid]
        new = sweep(mid, east, west, north, south, plane(first_ref, up), plane(first_ref, down))
        for c in range(3):
            second_ref[c, z] = jnp.where(keep, new[c], 0.0)
        return carry

    lax.fori_loop(0, layers, step_one, 0)

    def inner(values):
        return [v[0:rows, 0:columns] for v in values]

    def step_two(z, carry):
        up, down = lax.rem(z + 1, layers), lax.rem(z + layers - 1, layers)
        mid = plane(second_ref, z)
        east = inner([pltpu.roll(m[:, 0:columns], tall - 1, 0) for m in mid])
        west = inner([pltpu.roll(m[:, 0:columns], 1, 0) for m in mid])
        north = inner([pltpu.roll(m[0:rows], wide - 1, 1) for m in mid])
        south = inner([pltpu.roll(m[0:rows], 1, 1) for m in mid])
        above, below = inner(plane(second_ref, up)), inner(plane(second_ref, down))
        new = sweep(inner(mid), east, west, north, south, above, below)
        for c in range(3):
            last_ref[c, z] = new[c]
        return carry

    def store(n):
        span = pl.ds(n * chunk, chunk)
        return pltpu.make_async_copy(
            last_ref.at[:, span], fluid_ref.at[:, span], out_sem.at[n])

    slots = jnp.concatenate([table_ref[:, 0, :][:, p:p + 1] for p in range(per_owner)], axis=0)
    cells = chunk * rows
    for n in range(chunks):
        lax.fori_loop(n * chunk, (n + 1) * chunk, step_two, 0)
        store(n).start()
        taking = (iota((total, cells), 1) + n * cells == slots).astype(F32).astype(BF16)
        for c in range(3):
            flat = last_ref[c, n * chunk:(n + 1) * chunk].reshape(cells, columns).astype(BF16)
            part = jnp.dot(taking, flat, preferred_element_type=F32)
            sum_ref[c] = part if n == 0 else sum_ref[c] + part
    width = 3 * tiles * per_owner
    for c in range(3):
        for p in range(per_owner):
            for t in range(tiles):
                stage_ref[pl.ds(p * 3 * tiles + c * tiles + t, devices, stride=width), :] = (
                    sum_ref[c, p * devices:(p + 1) * devices, t * LANES:(t + 1) * LANES]
                )
    replies_ref[...] = stage_ref[...].reshape(replies_ref.shape).astype(BF16)
    for n in range(chunks):
        store(n).wait()


def gather_kernel(
    devices, per_owner, returned_ref, owners_ref, points_ref, weights_ref,
    out_ref, stage_ref, picked_ref,
):
    b = pl.program_id(0)
    k, points, patch = weights_ref.shape[1:]
    tiles = patch // LANES
    total = devices * per_owner

    @pl.when(b == 0)
    def _():
        stage_ref[...] = returned_ref[...].astype(F32).reshape(stage_ref.shape)
        owner_row = owners_ref[...]
        owner_column = to_column(owner_row)
        places = slot_column(owner_row, owner_column, devices)
        selector = (iota((places.shape[0], total), 1) == places).astype(F32).astype(BF16)
        for c in range(3):
            replies = unpack(stage_ref, devices, per_owner, tiles, c).astype(BF16)
            picked_ref[c] = jnp.dot(selector, replies, preferred_element_type=F32)

    span = pl.ds(pl.multiple_of(b * k, k), k)
    rows = [picked_ref[c, span, :] for c in range(3)]
    rows.append(jnp.zeros_like(rows[0]))
    left = jnp.concatenate(rows, axis=0).astype(BF16)
    right = weights_ref[0].reshape(k * points, patch)
    result = lax.dot_general(
        left, right, (((1,), (1,)), ((), ())), preferred_element_type=F32)
    diagonal = iota((k, k * points), 0) == iota((k, k * points), 1) // points
    for c in range(3):
        own = jnp.where(diagonal, result[c * k:(c + 1) * k], 0.0)
        fold = own[:, 0:points]
        for n in range(1, k):
            fold = fold + own[:, n * points:(n + 1) * points]
        interp = jnp.sum(fold, axis=0, keepdims=True)
        out_ref[0, c:c + 1, :] = points_ref[0, c:c + 1, :] + fiber_step * interp


def shards(rows_grid, columns_grid, velocity, fiber_points, stiffness, links, delta_weights,
           owners, patch_slots):
    blocks, intersection, points, patch = delta_weights.shape
    _, layers, rows, columns = velocity.shape
    devices = rows_grid * columns_grid
    entries = blocks * intersection
    per_owner = max(2, (2 * entries + devices - 1) // devices)
    total = devices * per_owner
    tiles = patch // LANES
    width = 3 * tiles * per_owner
    owner_row = owners.reshape(1, entries)
    slots_row = patch_slots.reshape(1, entries)
    whole = lambda shape: pl.BlockSpec(shape, lambda i: (0,) * len(shape))
    weight_spec = pl.BlockSpec((1, intersection, points, patch), lambda b: (b, 0, 0, 0))

    message = jax.ShapeDtypeStruct((devices, width, LANES), BF16)
    table_shape = jax.ShapeDtypeStruct((devices, 1, LANES), I32)
    stage = pltpu.VMEM((devices * width, LANES), F32)
    outgoing, table = pl.pallas_call(
        functools.partial(spread_kernel, devices, per_owner),
        grid=(blocks,),
        out_shape=[message, table_shape],
        in_specs=[
            whole(fiber_points.shape), whole((blocks, 1)), whole(links.shape),
            whole((1, entries)), whole((1, entries)), weight_spec,
        ],
        out_specs=[whole(message.shape), whole(table_shape.shape)],
        scratch_shapes=[
            pltpu.VMEM((3, blocks, points), F32), pltpu.VMEM((3, entries, patch), F32), stage,
        ],
    )(fiber_points, stiffness.reshape(blocks, 1), links, owner_row, slots_row, delta_weights)

    received, slots = swap([outgoing, table], rows_grid, columns_grid, 0)

    depth = 8
    sides_shape = (2, 3, 2, layers, columns)
    u, sides, ends, corners = pl.pallas_call(
        functools.partial(add_kernel, devices, per_owner),
        grid=(layers // depth,),
        out_shape=[
            jax.ShapeDtypeStruct(velocity.shape, F32),
            jax.ShapeDtypeStruct(sides_shape, BF16),
            jax.ShapeDtypeStruct((3, 16, layers * rows), BF16),
            jax.ShapeDtypeStruct((3, 16, LANES), BF16),
        ],
        in_specs=[
            whole(message.shape), whole(table_shape.shape),
            pl.BlockSpec((3, depth, rows, columns), lambda i: (0, i, 0, 0)),
        ],
        out_specs=[
            pl.BlockSpec((3, depth, rows, columns), lambda i: (0, i, 0, 0)),
            whole(sides_shape),
            pl.BlockSpec((3, 16, depth * rows), lambda i: (0, 0, i)),
            whole((3, 16, LANES)),
        ],
        scratch_shapes=[
            stage, pltpu.VMEM((3, total, patch), BF16), pltpu.VMEM(sides_shape, F32),
            pltpu.VMEM((3, 16, LANES), F32),
        ],
    )(received, slots, velocity)

    sides, ends, corners = pl.pallas_call(
        functools.partial(halo_kernel, rows_grid, columns_grid),
        out_shape=[
            jax.ShapeDtypeStruct(sides.shape, BF16),
            jax.ShapeDtypeStruct((2,) + ends.shape, BF16),
            jax.ShapeDtypeStruct((4,) + corners.shape, BF16),
        ],
        in_specs=[VMEM] * 3,
        out_specs=[VMEM] * 3,
        scratch_shapes=[pltpu.SemaphoreType.DMA((8,)), pltpu.SemaphoreType.DMA((8,))],
        compiler_params=pltpu.CompilerParams(collective_id=1, has_side_effects=True),
    )(sides, ends, corners)

    gx, gy = lax.axis_index("gx"), lax.axis_index("gy")
    flags = jnp.stack([gx > 0, gx < rows_grid - 1, gy > 0, gy < columns_grid - 1]).astype(I32)
    chunk = depth
    extended = (3, layers, rows + 8, columns + LANES)
    fluid, replies = pl.pallas_call(
        functools.partial(sweeps_kernel, devices, per_owner, chunk),
        out_shape=[jax.ShapeDtypeStruct(velocity.shape, F32), message],
        in_specs=[SMEM, VMEM, VMEM, VMEM, VMEM, ANY],
        out_specs=[ANY, VMEM],
        scratch_shapes=[
            pltpu.VMEM(extended, F32), pltpu.VMEM(extended, F32), pltpu.VMEM(velocity.shape, F32),
            pltpu.VMEM((2, 3, 2, layers, columns + LANES), F32), stage,
            pltpu.VMEM((3, total, patch), F32),
            pltpu.SemaphoreType.DMA((layers // chunk,)),
            pltpu.SemaphoreType.DMA((layers // chunk,)),
        ],
    )(flags, sides, ends, corners, slots, u)

    (returned,) = swap([replies], rows_grid, columns_grid, 2)

    moved = pl.pallas_call(
        functools.partial(gather_kernel, devices, per_owner),
        grid=(blocks,),
        out_shape=jax.ShapeDtypeStruct(fiber_points.shape, F32),
        in_specs=[
            whole(message.shape), whole((1, entries)),
            pl.BlockSpec((1, 3, points), lambda b: (b, 0, 0)), weight_spec,
        ],
        out_specs=pl.BlockSpec((1, 3, points), lambda b: (b, 0, 0)),
        scratch_shapes=[stage, pltpu.VMEM((3, entries, patch), F32)],
    )(returned, owner_row, fiber_points, delta_weights)
    return fluid, moved


def solution(mesh):
    placed = (
        P(None, None, "gx", "gy"),
        P(("gx", "gy"), None, None),
        P(("gx", "gy")),
        P(("gx", "gy"), None),
        P(("gx", "gy"), None, None, None),
        P(("gx", "gy"), None, None),
        P(("gx", "gy"), None),
    )
    return jax.shard_map(
        functools.partial(shards, mesh.shape["gx"], mesh.shape["gy"]),
        mesh=mesh,
        in_specs=placed,
        out_specs=(placed[0], placed[1]),
        check_vma=False,
    )
```

```python
import functools

import jax
import jax.numpy as jnp
from jax import lax
from jax.experimental import pallas as pl
from jax.experimental.pallas import tpu as pltpu
from jax.sharding import PartitionSpec as P

STEPS = 2
viscosity = 0.1
transport_rate = 0.1
force_step = 0.5
fiber_step = 0.25

F32 = jnp.float32
BF16 = jnp.bfloat16
I32 = jnp.int32
LANES = 128
MESH = pl.DeviceIdType.MESH
VMEM = pl.BlockSpec(memory_space=pltpu.VMEM)
ANY = pl.BlockSpec(memory_space=pl.ANY)
SMEM = pl.BlockSpec(memory_space=pltpu.SMEM)


def iota(shape, dim):
    return lax.broadcasted_iota(I32, shape, dim)


def to_column(row):
    n = row.shape[1]
    return jnp.sum(jnp.where(iota((n, n), 0) == iota((n, n), 1), row, 0), axis=1, keepdims=True)


def to_row(grid):
    n, k = grid.shape
    tiled = jnp.concatenate([grid] * n, axis=1)
    return jnp.sum(
        jnp.where(iota((n, n * k), 0) == iota((n, n * k), 1) // k, tiled, 0), axis=0, keepdims=True)


def slot_row(owner_row, owner_column, devices):
    n = owner_row.shape[1]
    same = (owner_column == owner_row) & (iota((n, n), 0) < iota((n, n), 1))
    rank = jnp.sum(jnp.where(same, 1, 0), axis=0, keepdims=True)
    return rank * devices + owner_row


def slot_column(owner_row, owner_column, devices):
    n = owner_row.shape[1]
    same = (owner_column == owner_row) & (iota((n, n), 1) < iota((n, n), 0))
    rank = jnp.sum(jnp.where(same, 1, 0), axis=1, keepdims=True)
    return rank * devices + owner_column


def spread_kernel(
    devices, per_owner, points_ref, stiffness_ref, links_ref, owners_ref, slots_ref, weights_ref,
    out_ref, table_ref, force_ref, contrib_ref, stage_ref,
):
    b = pl.program_id(0)
    blocks = pl.num_programs(0)
    k, points, patch = weights_ref.shape[1:]

    @pl.when(b == 0)
    def _():
        partner = lax.rem(iota(links_ref.shape, 1) + links_ref[...], points)
        for c in range(3):
            here = points_ref[c]
            there = jnp.take_along_axis(here, partner, axis=1)
            force_ref[c] = there - here

    diagonal = iota((k, k * points), 0) == iota((k, k * points), 1) // points
    rows = []
    for c in range(3):
        row = stiffness_ref[b] * force_ref[c, pl.ds(b, 1), :]
        rows.append(jnp.where(diagonal, jnp.concatenate([row] * k, axis=1), 0.0))
    rows.append(jnp.zeros_like(rows[0]))
    left = jnp.concatenate(rows, axis=0).astype(BF16)
    right = weights_ref[0].reshape(k * points, patch)
    result = jnp.dot(left, right, preferred_element_type=F32)
    for c in range(3):
        contrib_ref[c, pl.ds(pl.multiple_of(b * k, k), k), :] = result[c * k:(c + 1) * k]

    @pl.when(b == blocks - 1)
    def _():
        owner_row = to_row(owners_ref[:, 0, :])
        owner_column = to_column(owner_row)
        places = slot_row(owner_row, owner_column, devices)
        total = devices * per_owner
        chosen = iota((total, places.shape[1]), 0) == places
        selector = chosen.astype(F32).astype(BF16)
        tiles = patch // LANES
        width = 3 * tiles * per_owner
        for c in range(3):
            packed = jnp.dot(selector, contrib_ref[c].astype(BF16), preferred_element_type=F32)
            for p in range(per_owner):
                for t in range(tiles):
                    stage_ref[pl.ds(p * 3 * tiles + c * tiles + t, devices, stride=width), :] = (
                        packed[p * devices:(p + 1) * devices, t * LANES:(t + 1) * LANES]
                    )
        out_ref[...] = stage_ref[...].reshape(out_ref.shape).astype(BF16)
        column = jnp.max(jnp.where(chosen, to_row(slots_ref[...]), -1), axis=1, keepdims=True)
        lane = iota((devices, LANES), 1)
        table = jnp.full((devices, LANES), -1, I32)
        for p in range(per_owner):
            table = jnp.where(lane == p, column[p * devices:(p + 1) * devices], table)
        for d in range(devices):
            table_ref[d] = table[d:d + 1]


def start_swap(rows, columns, ins, outs, send_sem, recv_sem, own_sem):
    devices = rows * columns
    count = len(ins)
    me = lax.axis_index("gx") * columns + lax.axis_index("gy")

    def place(d):
        return (d // columns, lax.rem(d, columns))

    barrier = pltpu.get_barrier_semaphore()

    def hello(off, carry):
        other = lax.rem(me + off, devices)
        pl.semaphore_signal(barrier, inc=1, device_id=place(other), device_id_type=MESH)
        return carry

    lax.fori_loop(1, devices, hello, 0)
    pl.semaphore_wait(barrier, devices - 1)

    def copy(n, off):
        other = lax.rem(me + off, devices)
        return pltpu.make_async_remote_copy(
            src_ref=ins[n].at[other], dst_ref=outs[n].at[me],
            send_sem=send_sem.at[n, off], recv_sem=recv_sem.at[n, off],
            device_id=place(other), device_id_type=MESH,
        )

    def start(off, carry):
        for n in range(count):
            copy(n, off).start()
        return carry

    def finish(off, carry):
        for n in range(count):
            copy(n, off).wait()
        return carry

    def own(n):
        return pltpu.make_async_copy(ins[n].at[me], outs[n].at[me], own_sem.at[n])

    lax.fori_loop(1, devices, start, 0)
    for n in range(count):
        own(n).start()

    def wait():
        for n in range(count):
            own(n).wait()
        lax.fori_loop(1, devices, finish, 0)

    return wait


def swap_sems(count, devices):
    return [
        pltpu.SemaphoreType.DMA((count, devices)),
        pltpu.SemaphoreType.DMA((count, devices)),
        pltpu.SemaphoreType.DMA((count,)),
    ]


def unpack(stage_ref, devices, per_owner, tiles, c):
    width = 3 * tiles * per_owner
    rows = []
    for p in range(per_owner):
        rows.append(jnp.concatenate(
            [stage_ref[pl.ds(p * 3 * tiles + c * tiles + t, devices, stride=width), :]
             for t in range(tiles)], axis=1))
    return jnp.concatenate(rows, axis=0)


def table_row(table_ref, devices, per_owner):
    total = devices * per_owner
    row = jnp.zeros((1, total), I32)
    for p in range(per_owner):
        column = table_ref[:, 0, :][:, p:p + 1]
        spot = iota((devices, total), 1) == p * devices + iota((devices, total), 0)
        row = row + jnp.sum(jnp.where(spot, column, 0), axis=0, keepdims=True)
    return row


def table_column(table_ref, per_owner):
    return jnp.concatenate([table_ref[:, 0, :][:, p:p + 1] for p in range(per_owner)], axis=0)


def one_hot(mask):
    return mask.astype(F32).astype(BF16)


def dispatch_kernel(
    rows_grid, columns_grid, per_owner, out_ref, outtable_ref, velocity_ref,
    received_ref, table_ref, sides_out, ends_out, corners_out,
    row_ref, end_ref, edge_ref, ends_ref, stage_ref, force_ref, sides_send, ends_send,
    corners_send, send_sem, recv_sem, own_sem, load_sem, hsend_sem, hrecv_sem,
):
    devices = rows_grid * columns_grid
    total = devices * per_owner
    _, layers, rows, columns = velocity_ref.shape
    tiles = columns // LANES
    cells = layers * rows
    loads = []
    for side in range(2):
        loads.append(pltpu.make_async_copy(
            velocity_ref.at[:, :, pl.ds(side * (rows - 8), 8), :], row_ref.at[side],
            load_sem.at[side]))
        loads.append(pltpu.make_async_copy(
            velocity_ref.at[:, :, :, pl.ds(side * (columns - LANES), LANES)], end_ref.at[side],
            load_sem.at[2 + side]))
    for load in loads:
        load.start()
    wait = start_swap(
        rows_grid, columns_grid, [out_ref, outtable_ref], [received_ref, table_ref],
        send_sem, recv_sem, own_sem)

    cell, want = iota((cells, LANES), 0), iota((cells, LANES), 1)
    z, x = cell // rows, lax.rem(cell, rows)
    edge_ref[...] = one_hot((x == 0) & (want == z) | (x == rows - 1) & (want == layers + z))
    r8, l8 = iota((8, LANES), 0), iota((8, LANES), 1)

    def pick(side, c):
        r = r8 - 2 * c
        return one_hot((r >= 0) & (r < 2) & (l8 == r + side * (LANES - 2)))

    for load in loads:
        load.wait()
    across = (((1,), (1,)), ((), ()))
    for side in range(2):
        found = jnp.zeros((8, cells), F32)
        for c in range(3):
            flat = end_ref[side, c].reshape(cells, LANES)
            high = flat.astype(BF16)
            low = (flat - high.astype(F32)).astype(BF16)
            for part in (high, low):
                found = found + lax.dot_general(
                    pick(side, c), part, across, preferred_element_type=F32)
        ends_ref[side] = found

    wait()

    stage_ref[...] = received_ref[...].astype(F32).reshape(stage_ref.shape)
    slots_row = table_row(table_ref, devices, per_owner)
    slots_column = table_column(table_ref, per_owner)
    e = iota((4 * layers, total), 0)
    line, z = e // layers, lax.rem(e, layers)
    x = jnp.where(line < 2, line, rows - 4 + line)
    placing = one_hot(z * rows + x == slots_row)
    for c in range(3):
        force = unpack(stage_ref, devices, per_owner, tiles, c).astype(BF16)
        force_ref[c] = force
        push = jnp.dot(placing, force, preferred_element_type=F32)
        for side in range(2):
            for r in range(2):
                n = side * 2 + r
                v = row_ref[side, c, :, 6 * side + r, :]
                v = v + force_step * push[n * layers:(n + 1) * layers]
                sides_send[side, c, r] = v.astype(BF16)

    gx, gy = lax.axis_index("gx"), lax.axis_index("gy")
    west, east, south, north = gx > 0, gx < rows_grid - 1, gy > 0, gy < columns_grid - 1
    plan = [
        (sides_send.at[0], sides_out.at[1], (-1, 0), west, east),
        (sides_send.at[1], sides_out.at[0], (1, 0), east, west),
        (ends_send.at[0], ends_out.at[1], (0, -1), south, north),
        (ends_send.at[1], ends_out.at[0], (0, 1), north, south),
        (corners_send.at[0], corners_out.at[3], (-1, -1), west & south, east & north),
        (corners_send.at[1], corners_out.at[2], (-1, 1), west & north, east & south),
        (corners_send.at[0], corners_out.at[1], (1, -1), east & south, west & north),
        (corners_send.at[1], corners_out.at[0], (1, 1), east & north, west & south),
    ]
    copies = []
    for n, (source, target, (dx, dy), _, _) in enumerate(plan):
        to = (lax.rem(gx + dx + rows_grid, rows_grid), lax.rem(gy + dy + columns_grid, columns_grid))
        copies.append(pltpu.make_async_remote_copy(
            src_ref=source, dst_ref=target, send_sem=hsend_sem.at[n], recv_sem=hrecv_sem.at[n],
            device_id=to, device_id_type=MESH))

    def go(n):
        @pl.when(plan[n][3])
        def _():
            copies[n].start()

    go(0)
    go(1)
    taking = one_hot(iota((total, cells), 1) == slots_column)
    for side in range(2):
        first = side * (columns - LANES)
        mine = jnp.zeros((8, total), F32)
        for c in range(3):
            mine = mine + lax.dot_general(
                pick(side, c), force_ref[c, :, first:first + LANES], across,
                preferred_element_type=F32)
        push = jnp.dot(mine.astype(BF16), taking, preferred_element_type=F32)
        ends = (ends_ref[side] + force_step * push).astype(BF16)
        ends_send[side] = ends
        corners_send[side] = jnp.dot(
            ends, edge_ref[...], preferred_element_type=F32).astype(BF16)
    for n in range(2, 8):
        go(n)
    for n in range(8):
        @pl.when(plan[n][3])
        def _():
            copies[n].wait_send()

        @pl.when(plan[n][4])
        def _():
            copies[n].wait_recv()


def sweep(mid, east, west, north, south, above, below):
    r = transport_rate
    coefficients = [(viscosity - r * m, viscosity + r * m) for m in mid]
    keep = 1.0 - 6.0 * viscosity
    out = []
    for c in range(3):
        v = keep * mid[c]
        for (ahead, behind), (front, back) in zip(
            coefficients, ((east, west), (north, south), (above, below))
        ):
            v = v + (ahead * front[c] + behind * back[c])
        out.append(v)
    return out


def sweeps_kernel(
    devices, per_owner, rows_grid, columns_grid, chunk, sides_ref, ends_ref, corners_ref,
    table_ref, received_ref, velocity_ref,
    fluid_ref, replies_ref, first_ref, second_ref, last_ref, side_ref, stage_ref, sum_ref,
    force_ref, in_sem, out_sem,
):
    _, layers, rows, columns = velocity_ref.shape
    tiles = columns // LANES
    total = devices * per_owner
    chunks = layers // chunk
    cells = chunk * rows
    tall, wide = rows + 8, columns + LANES

    def load(n):
        span = pl.ds(n * chunk, chunk)
        return pltpu.make_async_copy(
            velocity_ref.at[:, span], first_ref.at[:, span, 0:rows, 0:columns], in_sem.at[n])

    for n in range(chunks):
        load(n).start()

    gx, gy = lax.axis_index("gx"), lax.axis_index("gy")
    has = [gx > 0, gx < rows_grid - 1, gy > 0, gy < columns_grid - 1]
    for side in range(2):
        side_ref[side, :, :, :, 0:columns] = jnp.where(has[side], sides_ref[side].astype(F32), 0.0)
        side_ref[side, :, :, :, columns:] = jnp.zeros((3, 2, layers, LANES), F32)
    r8, l8 = iota((8, LANES), 0), iota((8, LANES), 1)

    def expand(ref, n, side, c, there):
        r = r8 - 2 * c
        pick = one_hot((r >= 0) & (r < 2) & (l8 == r + (1 - side) * (LANES - 2)))
        values = jnp.where(there, ref[n].astype(F32), 0.0).astype(BF16)
        return lax.dot_general(
            values, pick, (((0,), (0,)), ((), ())), preferred_element_type=F32)

    for c in range(3):
        band = expand(ends_ref, 0, 0, c, has[2]) + expand(ends_ref, 1, 1, c, has[3])
        first_ref[c, :, 0:rows, columns:] = band.reshape(layers, rows, LANES)
        low = expand(corners_ref, 0, 0, c, has[0] & has[2])
        low = low + expand(corners_ref, 1, 1, c, has[0] & has[3])
        high = expand(corners_ref, 2, 0, c, has[1] & has[2])
        high = high + expand(corners_ref, 3, 1, c, has[1] & has[3])
        side_ref[0, c, 1, :, columns:] = low[layers:2 * layers]
        side_ref[1, c, 0, :, columns:] = high[0:layers]

    wide8 = iota((8, wide), 0)

    def border(z, carry):
        for c in range(3):
            tile = jnp.zeros((8, wide), F32)
            for place, side, r in ((0, 1, 0), (1, 1, 1), (6, 0, 0), (7, 0, 1)):
                tile = jnp.where(wide8 == place, side_ref[side, c, r, pl.ds(z, 1), :], tile)
            first_ref[c, pl.ds(z, 1), rows:, :] = tile[None]
        return carry

    lax.fori_loop(0, layers, border, 0)

    stage_ref[...] = received_ref[...].astype(F32).reshape(stage_ref.shape)
    for c in range(3):
        force_ref[c] = (force_step * unpack(stage_ref, devices, per_owner, tiles, c)).astype(BF16)
    slots_row = table_row(table_ref, devices, per_owner)
    for n in range(chunks):
        load(n).wait()
        placing = one_hot(iota((cells, total), 0) + n * cells == slots_row)
        span = slice(n * chunk, (n + 1) * chunk)
        for c in range(3):
            push = jnp.dot(placing, force_ref[c], preferred_element_type=F32)
            first_ref[c, span, 0:rows, 0:columns] += push.reshape(chunk, rows, columns)

    lane8 = iota((8, wide), 1)
    lane_keep = (lane8 < columns) | (lane8 == columns) & has[3] | (lane8 == wide - 1) & has[2]
    row_keep = (wide8 == 0) & has[1] | (wide8 == 7) & has[0]

    def tile(ref, c, z, t, width):
        return ref[c, z, 8 * t:8 * t + 8, 0:width]

    def neighbours(ref, z, t, width):
        count = tall // 8
        up, down = lax.rem(z + 1, layers), lax.rem(z + layers - 1, layers)
        row = wide8[:, 0:width]
        out = []
        for c in range(3):
            full = tile(ref, c, z, t, wide)
            mid = full[:, 0:width]
            after = tile(ref, c, z, (t + 1) % count, width)
            before = tile(ref, c, z, (t + count - 1) % count, width)
            east = pltpu.roll(jnp.where(row == 0, after, mid), 7, 0)
            west = pltpu.roll(jnp.where(row == 7, before, mid), 1, 0)
            north = pltpu.roll(full, wide - 1, 1)[:, 0:width]
            south = pltpu.roll(full, 1, 1)[:, 0:width]
            out.append((
                mid, east, west, north, south, tile(ref, c, up, t, width),
                tile(ref, c, down, t, width)))
        return [list(v) for v in zip(*out)]

    def step_one(z, carry):
        for t in range(tall // 8):
            new = sweep(*neighbours(first_ref, z, t, wide))
            keep = lane_keep if t < rows // 8 else lane_keep & row_keep
            for c in range(3):
                second_ref[c, z, 8 * t:8 * t + 8, :] = jnp.where(keep, new[c], 0.0)
        return carry

    lax.fori_loop(0, layers, step_one, 0)

    def step_two(z, carry):
        for t in range(rows // 8):
            new = sweep(*neighbours(second_ref, z, t, columns))
            for c in range(3):
                last_ref[c, z, 8 * t:8 * t + 8, :] = new[c]
        return carry

    def store(n):
        span = pl.ds(n * chunk, chunk)
        return pltpu.make_async_copy(
            last_ref.at[:, span], fluid_ref.at[:, span], out_sem.at[n])

    slots = table_column(table_ref, per_owner)
    for n in range(chunks):
        lax.fori_loop(n * chunk, (n + 1) * chunk, step_two, 0)
        store(n).start()
        taking = one_hot(iota((total, cells), 1) + n * cells == slots)
        for c in range(3):
            flat = last_ref[c, n * chunk:(n + 1) * chunk].reshape(cells, columns).astype(BF16)
            part = jnp.dot(taking, flat, preferred_element_type=F32)
            sum_ref[c] = part if n == 0 else sum_ref[c] + part
    width = 3 * tiles * per_owner
    for c in range(3):
        for p in range(per_owner):
            for t in range(tiles):
                stage_ref[pl.ds(p * 3 * tiles + c * tiles + t, devices, stride=width), :] = (
                    sum_ref[c, p * devices:(p + 1) * devices, t * LANES:(t + 1) * LANES]
                )
    replies_ref[...] = stage_ref[...].reshape(replies_ref.shape).astype(BF16)
    for n in range(chunks):
        store(n).wait()


def gather_kernel(
    rows_grid, columns_grid, per_owner, replies_ref, owners_ref, points_ref, weights_ref,
    out_ref, returned_ref, loaded_ref, stage_ref, picked_ref, send_sem, recv_sem, own_sem, load_sem,
):
    devices = rows_grid * columns_grid
    blocks, k, points, patch = weights_ref.shape
    tiles = patch // LANES
    total = devices * per_owner

    def load(b):
        return pltpu.make_async_copy(weights_ref.at[b], loaded_ref.at[b], load_sem.at[b])

    for b in range(blocks):
        load(b).start()
    wait = start_swap(
        rows_grid, columns_grid, [replies_ref], [returned_ref], send_sem, recv_sem, own_sem)
    owner_row = to_row(owners_ref[:, 0, :])
    places = slot_column(owner_row, to_column(owner_row), devices)
    selector = one_hot(iota((places.shape[0], total), 1) == places)
    for b in range(blocks):
        load(b).wait()
    wait()
    stage_ref[...] = returned_ref[...].astype(F32).reshape(stage_ref.shape)
    for c in range(3):
        replies = unpack(stage_ref, devices, per_owner, tiles, c).astype(BF16)
        picked_ref[c] = jnp.dot(selector, replies, preferred_element_type=F32)
    diagonal = iota((k, k * points), 0) == iota((k, k * points), 1) // points
    for b in range(blocks):
        rows = [picked_ref[c, b * k:(b + 1) * k, :] for c in range(3)]
        rows.append(jnp.zeros_like(rows[0]))
        left = jnp.concatenate(rows, axis=0).astype(BF16)
        right = loaded_ref[b].reshape(k * points, patch)
        result = lax.dot_general(
            left, right, (((1,), (1,)), ((), ())), preferred_element_type=F32)
        for c in range(3):
            own = jnp.where(diagonal, result[c * k:(c + 1) * k], 0.0)
            fold = own[:, 0:points]
            for n in range(1, k):
                fold = fold + own[:, n * points:(n + 1) * points]
            interp = jnp.sum(fold, axis=0, keepdims=True)
            out_ref[c, b:b + 1, :] = points_ref[c, b:b + 1, :] + fiber_step * interp


def shards(rows_grid, columns_grid, velocity, fiber_points, stiffness, links, delta_weights,
           owners, patch_slots):
    blocks, intersection, points, patch = delta_weights.shape
    _, layers, rows, columns = velocity.shape
    devices = rows_grid * columns_grid
    entries = blocks * intersection
    per_owner = max(2, (2 * entries + devices - 1) // devices)
    total = devices * per_owner
    tiles = patch // LANES
    width = 3 * tiles * per_owner
    owners = jnp.transpose(owners, (0, 2, 1))
    points_first = jnp.transpose(fiber_points, (1, 0, 2))
    whole = lambda shape: pl.BlockSpec(shape, lambda i: (0,) * len(shape))
    message = jax.ShapeDtypeStruct((devices, width, LANES), BF16)
    table_shape = jax.ShapeDtypeStruct((devices, 1, LANES), I32)
    stage = pltpu.VMEM((devices * width, LANES), F32)
    outgoing, table = pl.pallas_call(
        functools.partial(spread_kernel, devices, per_owner),
        grid=(blocks,),
        out_shape=[message, table_shape],
        in_specs=[
            whole(points_first.shape), SMEM, whole(links.shape), whole(owners.shape),
            whole(patch_slots.shape),
            pl.BlockSpec((1, intersection, points, patch), lambda b: (b, 0, 0, 0)),
        ],
        out_specs=[whole(message.shape), whole(table_shape.shape)],
        scratch_shapes=[
            pltpu.VMEM((3, blocks, points), F32), pltpu.VMEM((3, entries, patch), F32), stage,
        ],
    )(points_first, stiffness, links, owners, patch_slots, delta_weights)

    sides_shape = (2, 3, 2, layers, columns)
    ends_shape = (2, 8, layers * rows)
    received, slots, sides, ends, corners = pl.pallas_call(
        functools.partial(dispatch_kernel, rows_grid, columns_grid, per_owner),
        out_shape=[
            message, table_shape,
            jax.ShapeDtypeStruct(sides_shape, BF16),
            jax.ShapeDtypeStruct(ends_shape, BF16),
            jax.ShapeDtypeStruct((4, 8, LANES), BF16),
        ],
        in_specs=[VMEM, VMEM, ANY],
        out_specs=[VMEM] * 5,
        scratch_shapes=[
            pltpu.VMEM((2, 3, layers, 8, columns), F32),
            pltpu.VMEM((2, 3, layers, rows, LANES), F32),
            pltpu.VMEM((layers * rows, LANES), BF16),
            pltpu.VMEM(ends_shape, F32),
            stage,
            pltpu.VMEM((3, total, patch), BF16),
            pltpu.VMEM(sides_shape, BF16),
            pltpu.VMEM(ends_shape, BF16),
            pltpu.VMEM((2, 8, LANES), BF16),
            *swap_sems(2, devices),
            pltpu.SemaphoreType.DMA((4,)),
            pltpu.SemaphoreType.DMA((8,)),
            pltpu.SemaphoreType.DMA((8,)),
        ],
        compiler_params=pltpu.CompilerParams(collective_id=0, has_side_effects=True),
    )(outgoing, table, velocity)

    chunk = 8
    extended = (3, layers, rows + 8, columns + LANES)
    fluid, replies = pl.pallas_call(
        functools.partial(sweeps_kernel, devices, per_owner, rows_grid, columns_grid, chunk),
        out_shape=[jax.ShapeDtypeStruct(velocity.shape, F32), message],
        in_specs=[VMEM] * 5 + [ANY],
        out_specs=[ANY, VMEM],
        scratch_shapes=[
            pltpu.VMEM(extended, F32), pltpu.VMEM(extended, F32), pltpu.VMEM(velocity.shape, F32),
            pltpu.VMEM((2, 3, 2, layers, columns + LANES), F32), stage,
            pltpu.VMEM((3, total, patch), F32), pltpu.VMEM((3, total, patch), BF16),
            pltpu.SemaphoreType.DMA((layers // chunk,)),
            pltpu.SemaphoreType.DMA((layers // chunk,)),
        ],
    )(sides, ends, corners, slots, received, velocity)

    moved = pl.pallas_call(
        functools.partial(gather_kernel, rows_grid, columns_grid, per_owner),
        out_shape=jax.ShapeDtypeStruct(points_first.shape, F32),
        in_specs=[VMEM, VMEM, VMEM, ANY],
        out_specs=VMEM,
        scratch_shapes=[
            pltpu.VMEM(message.shape, BF16), pltpu.VMEM(delta_weights.shape, BF16), stage,
            pltpu.VMEM((3, entries, patch), F32), *swap_sems(1, devices),
            pltpu.SemaphoreType.DMA((blocks,)),
        ],
        compiler_params=pltpu.CompilerParams(collective_id=1, has_side_effects=True),
    )(replies, owners, points_first, delta_weights)
    return fluid, jnp.transpose(moved, (1, 0, 2))


def solution(mesh):
    placed = (
        P(None, None, "gx", "gy"),
        P(("gx", "gy"), None, None),
        P(("gx", "gy")),
        P(("gx", "gy"), None),
        P(("gx", "gy"), None, None, None),
        P(("gx", "gy"), None, None),
        P(("gx", "gy"), None),
    )
    return jax.shard_map(
        functools.partial(shards, mesh.shape["gx"], mesh.shape["gy"]),
        mesh=mesh,
        in_specs=placed,
        out_specs=(placed[0], placed[1]),
        check_vma=False,
    )
```

```python
import functools

import jax
import jax.numpy as jnp
from jax import lax
from jax.experimental import pallas as pl
from jax.experimental.pallas import tpu as pltpu
from jax.sharding import PartitionSpec as P

STEPS = 2
viscosity = 0.1
transport_rate = 0.1
force_step = 0.5
fiber_step = 0.25

F32 = jnp.float32
BF16 = jnp.bfloat16
I32 = jnp.int32
LANES = 128
MESH = pl.DeviceIdType.MESH
VMEM = pl.BlockSpec(memory_space=pltpu.VMEM)
ANY = pl.BlockSpec(memory_space=pl.ANY)
SMEM = pl.BlockSpec(memory_space=pltpu.SMEM)


def iota(shape, dim):
    return lax.broadcasted_iota(I32, shape, dim)


def to_column(row):
    n = row.shape[1]
    return jnp.sum(jnp.where(iota((n, n), 0) == iota((n, n), 1), row, 0), axis=1, keepdims=True)


def to_row(grid):
    n, k = grid.shape
    tiled = jnp.concatenate([grid] * n, axis=1)
    return jnp.sum(
        jnp.where(iota((n, n * k), 0) == iota((n, n * k), 1) // k, tiled, 0), axis=0, keepdims=True)


def slot_row(owner_row, owner_column, devices):
    n = owner_row.shape[1]
    same = (owner_column == owner_row) & (iota((n, n), 0) < iota((n, n), 1))
    rank = jnp.sum(jnp.where(same, 1, 0), axis=0, keepdims=True)
    return rank * devices + owner_row


def slot_column(owner_row, owner_column, devices):
    n = owner_row.shape[1]
    same = (owner_column == owner_row) & (iota((n, n), 1) < iota((n, n), 0))
    rank = jnp.sum(jnp.where(same, 1, 0), axis=1, keepdims=True)
    return rank * devices + owner_column


def spread(
    devices, per_owner, points_ref, stiffness_ref, links_ref, owners_ref, slots_ref, loaded_ref,
    out_ref, table_ref, contrib_ref, stage_ref, wait_block,
):
    blocks, k, points, patch = loaded_ref.shape
    parts = []
    for c in range(3):
        rest = points_ref[c]
        for _ in range(3):
            part = rest.astype(BF16).astype(F32)
            parts.append(part)
            rest = rest - part
    parts.append(jnp.zeros_like(parts[0]))
    parts = jnp.concatenate(parts, axis=0).astype(BF16)
    partner = lax.rem(iota(links_ref.shape, 1) + links_ref[...], points)
    diagonal = iota((k, k * points), 0) == iota((k, k * points), 1) // points
    lefts = []
    for b in range(blocks):
        moving = one_hot(iota((points, points), 0) == partner[b:b + 1])
        there = jnp.dot(parts, moving, preferred_element_type=F32)
        rows = []
        for c in range(3):
            r = 3 * c * blocks + b
            found = there[r:r + 1] + there[r + blocks:r + blocks + 1]
            found = found + there[r + 2 * blocks:r + 2 * blocks + 1]
            row = stiffness_ref[b] * (found - points_ref[c, b:b + 1, :])
            rows.append(jnp.where(diagonal, jnp.concatenate([row] * k, axis=1), 0.0))
        rows.append(jnp.zeros_like(rows[0]))
        lefts.append(jnp.concatenate(rows, axis=0).astype(BF16))

    owner_row = to_row(owners_ref[:, 0, :])
    places = slot_row(owner_row, to_column(owner_row), devices)
    total = devices * per_owner
    chosen = iota((total, places.shape[1]), 0) == places
    selector = one_hot(chosen)

    for b in range(blocks):
        wait_block(b)
        right = loaded_ref[b].reshape(k * points, patch)
        result = jnp.dot(lefts[b], right, preferred_element_type=F32)
        for c in range(3):
            contrib_ref[c, b * k:(b + 1) * k, :] = result[c * k:(c + 1) * k]

    tiles = patch // LANES
    width = 3 * tiles * per_owner
    for c in range(3):
        packed = jnp.dot(selector, contrib_ref[c].astype(BF16), preferred_element_type=F32)
        for p in range(per_owner):
            for t in range(tiles):
                stage_ref[pl.ds(p * 3 * tiles + c * tiles + t, devices, stride=width), :] = (
                    packed[p * devices:(p + 1) * devices, t * LANES:(t + 1) * LANES]
                )
    out_ref[...] = stage_ref[...].reshape(out_ref.shape).astype(BF16)
    column = jnp.max(jnp.where(chosen, to_row(slots_ref[...]), -1), axis=1, keepdims=True)
    lane = iota((devices, LANES), 1)
    table = jnp.full((devices, LANES), -1, I32)
    for p in range(per_owner):
        table = jnp.where(lane == p, column[p * devices:(p + 1) * devices], table)
    for d in range(devices):
        table_ref[d] = table[d:d + 1]


def start_swap(rows, columns, ins, outs, send_sem, recv_sem, own_sem, prepare=None):
    devices = rows * columns
    count = len(ins)
    me = lax.axis_index("gx") * columns + lax.axis_index("gy")

    def place(d):
        return (d // columns, lax.rem(d, columns))

    barrier = pltpu.get_barrier_semaphore()

    def hello(off, carry):
        other = lax.rem(me + off, devices)
        pl.semaphore_signal(barrier, inc=1, device_id=place(other), device_id_type=MESH)
        return carry

    lax.fori_loop(1, devices, hello, 0)
    if prepare is not None:
        prepare()
    pl.semaphore_wait(barrier, devices - 1)

    def copy(n, off):
        other = lax.rem(me + off, devices)
        return pltpu.make_async_remote_copy(
            src_ref=ins[n].at[other], dst_ref=outs[n].at[me],
            send_sem=send_sem.at[n, off], recv_sem=recv_sem.at[n, off],
            device_id=place(other), device_id_type=MESH,
        )

    def start(off, carry):
        for n in range(count):
            copy(n, off).start()
        return carry

    def finish(off, carry):
        for n in range(count):
            copy(n, off).wait()
        return carry

    def own(n):
        return pltpu.make_async_copy(ins[n].at[me], outs[n].at[me], own_sem.at[n])

    lax.fori_loop(1, devices, start, 0)
    for n in range(count):
        own(n).start()

    def wait():
        for n in range(count):
            own(n).wait()
        lax.fori_loop(1, devices, finish, 0)

    return wait


def swap_sems(count, devices):
    return [
        pltpu.SemaphoreType.DMA((count, devices)),
        pltpu.SemaphoreType.DMA((count, devices)),
        pltpu.SemaphoreType.DMA((count,)),
    ]


def unpack(stage_ref, devices, per_owner, tiles, c):
    width = 3 * tiles * per_owner
    rows = []
    for p in range(per_owner):
        rows.append(jnp.concatenate(
            [stage_ref[pl.ds(p * 3 * tiles + c * tiles + t, devices, stride=width), :]
             for t in range(tiles)], axis=1))
    return jnp.concatenate(rows, axis=0)


def table_row(table_ref, devices, per_owner):
    total = devices * per_owner
    row = jnp.zeros((1, total), I32)
    for p in range(per_owner):
        column = table_ref[:, 0, :][:, p:p + 1]
        spot = iota((devices, total), 1) == p * devices + iota((devices, total), 0)
        row = row + jnp.sum(jnp.where(spot, column, 0), axis=0, keepdims=True)
    return row


def table_column(table_ref, per_owner):
    return jnp.concatenate([table_ref[:, 0, :][:, p:p + 1] for p in range(per_owner)], axis=0)


def one_hot(mask):
    return mask.astype(F32).astype(BF16)


def dispatch_kernel(
    rows_grid, columns_grid, per_owner, points_ref, stiffness_ref, links_ref, owners_ref,
    slots_ref, weights_ref, velocity_ref,
    received_ref, table_ref, sides_out, ends_out, corners_out,
    out_ref, outtable_ref, loaded_ref, contrib_ref,
    row_ref, end_ref, edge_ref, ends_ref, stage_ref, force_ref, sides_send, ends_send,
    corners_send, send_sem, recv_sem, own_sem, load_sem, block_sem, hsend_sem, hrecv_sem,
):
    devices = rows_grid * columns_grid
    total = devices * per_owner
    _, layers, rows, columns = velocity_ref.shape
    tiles = columns // LANES
    cells = layers * rows
    loads = []
    for side in range(2):
        loads.append(pltpu.make_async_copy(
            velocity_ref.at[:, :, pl.ds(side * (rows - 8), 8), :], row_ref.at[side],
            load_sem.at[side]))
        loads.append(pltpu.make_async_copy(
            velocity_ref.at[:, :, :, pl.ds(side * (columns - LANES), LANES)], end_ref.at[side],
            load_sem.at[2 + side]))

    def block(b):
        return pltpu.make_async_copy(weights_ref.at[b], loaded_ref.at[b], block_sem.at[b])

    for b in range(weights_ref.shape[0]):
        block(b).start()
    for load in loads:
        load.start()

    def prepare():
        spread(
            devices, per_owner, points_ref, stiffness_ref, links_ref, owners_ref, slots_ref,
            loaded_ref, out_ref, outtable_ref, contrib_ref, stage_ref,
            lambda b: block(b).wait())

    wait = start_swap(
        rows_grid, columns_grid, [out_ref, outtable_ref], [received_ref, table_ref],
        send_sem, recv_sem, own_sem, prepare)

    cell, want = iota((cells, LANES), 0), iota((cells, LANES), 1)
    z, x = cell // rows, lax.rem(cell, rows)
    edge_ref[...] = one_hot((x == 0) & (want == z) | (x == rows - 1) & (want == layers + z))
    r8, l8 = iota((8, LANES), 0), iota((8, LANES), 1)

    def pick(side, c):
        r = r8 - 2 * c
        return one_hot((r >= 0) & (r < 2) & (l8 == r + side * (LANES - 2)))

    for load in loads:
        load.wait()
    across = (((1,), (1,)), ((), ()))
    for side in range(2):
        found = jnp.zeros((8, cells), F32)
        for c in range(3):
            flat = end_ref[side, c].reshape(cells, LANES)
            high = flat.astype(BF16)
            low = (flat - high.astype(F32)).astype(BF16)
            for part in (high, low):
                found = found + lax.dot_general(
                    pick(side, c), part, across, preferred_element_type=F32)
        ends_ref[side] = found

    wait()

    stage_ref[...] = received_ref[...].astype(F32).reshape(stage_ref.shape)
    slots_row = table_row(table_ref, devices, per_owner)
    slots_column = table_column(table_ref, per_owner)
    e = iota((4 * layers, total), 0)
    line, z = e // layers, lax.rem(e, layers)
    x = jnp.where(line < 2, line, rows - 4 + line)
    placing = one_hot(z * rows + x == slots_row)
    for c in range(3):
        force = unpack(stage_ref, devices, per_owner, tiles, c).astype(BF16)
        force_ref[c] = force
        push = jnp.dot(placing, force, preferred_element_type=F32)
        for side in range(2):
            for r in range(2):
                n = side * 2 + r
                v = row_ref[side, c, :, 6 * side + r, :]
                v = v + force_step * push[n * layers:(n + 1) * layers]
                sides_send[side, c, r] = v.astype(BF16)

    gx, gy = lax.axis_index("gx"), lax.axis_index("gy")
    west, east, south, north = gx > 0, gx < rows_grid - 1, gy > 0, gy < columns_grid - 1
    plan = [
        (sides_send.at[0], sides_out.at[1], (-1, 0), west, east),
        (sides_send.at[1], sides_out.at[0], (1, 0), east, west),
        (ends_send.at[0], ends_out.at[1], (0, -1), south, north),
        (ends_send.at[1], ends_out.at[0], (0, 1), north, south),
        (corners_send.at[0], corners_out.at[3], (-1, -1), west & south, east & north),
        (corners_send.at[1], corners_out.at[2], (-1, 1), west & north, east & south),
        (corners_send.at[0], corners_out.at[1], (1, -1), east & south, west & north),
        (corners_send.at[1], corners_out.at[0], (1, 1), east & north, west & south),
    ]
    copies = []
    for n, (source, target, (dx, dy), _, _) in enumerate(plan):
        to = (lax.rem(gx + dx + rows_grid, rows_grid), lax.rem(gy + dy + columns_grid, columns_grid))
        copies.append(pltpu.make_async_remote_copy(
            src_ref=source, dst_ref=target, send_sem=hsend_sem.at[n], recv_sem=hrecv_sem.at[n],
            device_id=to, device_id_type=MESH))

    def go(n):
        @pl.when(plan[n][3])
        def _():
            copies[n].start()

    go(0)
    go(1)
    taking = one_hot(iota((total, cells), 1) == slots_column)
    for side in range(2):
        first = side * (columns - LANES)
        mine = jnp.zeros((8, total), F32)
        for c in range(3):
            mine = mine + lax.dot_general(
                pick(side, c), force_ref[c, :, first:first + LANES], across,
                preferred_element_type=F32)
        push = jnp.dot(mine.astype(BF16), taking, preferred_element_type=F32)
        ends = (ends_ref[side] + force_step * push).astype(BF16)
        ends_send[side] = ends
        corners_send[side] = jnp.dot(
            ends, edge_ref[...], preferred_element_type=F32).astype(BF16)
    for n in range(2, 8):
        go(n)
    for n in range(8):
        @pl.when(plan[n][3])
        def _():
            copies[n].wait_send()

        @pl.when(plan[n][4])
        def _():
            copies[n].wait_recv()


def sweep(mid, east, west, north, south, above, below):
    r = transport_rate
    coefficients = [(viscosity - r * m, viscosity + r * m) for m in mid]
    keep = 1.0 - 6.0 * viscosity
    out = []
    for c in range(3):
        v = keep * mid[c]
        for (ahead, behind), (front, back) in zip(
            coefficients, ((east, west), (north, south), (above, below))
        ):
            v = v + (ahead * front[c] + behind * back[c])
        out.append(v)
    return out


def sweeps_kernel(
    devices, per_owner, rows_grid, columns_grid, chunk, sides_ref, ends_ref, corners_ref,
    table_ref, received_ref, velocity_ref,
    fluid_ref, replies_ref, first_ref, second_ref, last_ref, side_ref, stage_ref, sum_ref,
    force_ref, in_sem, out_sem,
):
    _, layers, rows, columns = velocity_ref.shape
    tiles = columns // LANES
    total = devices * per_owner
    chunks = layers // chunk
    cells = chunk * rows
    tall, wide = rows + 8, columns + LANES

    def load(n):
        span = pl.ds(n * chunk, chunk)
        return pltpu.make_async_copy(
            velocity_ref.at[:, span], first_ref.at[:, span, 0:rows, 0:columns], in_sem.at[n])

    for n in range(chunks):
        load(n).start()

    gx, gy = lax.axis_index("gx"), lax.axis_index("gy")
    has = [gx > 0, gx < rows_grid - 1, gy > 0, gy < columns_grid - 1]
    for side in range(2):
        side_ref[side, :, :, :, 0:columns] = jnp.where(has[side], sides_ref[side].astype(F32), 0.0)
        side_ref[side, :, :, :, columns:] = jnp.zeros((3, 2, layers, LANES), F32)
    r8, l8 = iota((8, LANES), 0), iota((8, LANES), 1)

    def expand(ref, n, side, c, there):
        r = r8 - 2 * c
        pick = one_hot((r >= 0) & (r < 2) & (l8 == r + (1 - side) * (LANES - 2)))
        values = jnp.where(there, ref[n].astype(F32), 0.0).astype(BF16)
        return lax.dot_general(
            values, pick, (((0,), (0,)), ((), ())), preferred_element_type=F32)

    for c in range(3):
        band = expand(ends_ref, 0, 0, c, has[2]) + expand(ends_ref, 1, 1, c, has[3])
        first_ref[c, :, 0:rows, columns:] = band.reshape(layers, rows, LANES)
        low = expand(corners_ref, 0, 0, c, has[0] & has[2])
        low = low + expand(corners_ref, 1, 1, c, has[0] & has[3])
        high = expand(corners_ref, 2, 0, c, has[1] & has[2])
        high = high + expand(corners_ref, 3, 1, c, has[1] & has[3])
        side_ref[0, c, 1, :, columns:] = low[layers:2 * layers]
        side_ref[1, c, 0, :, columns:] = high[0:layers]

    wide8 = iota((8, wide), 0)

    def border(z, carry):
        for c in range(3):
            tile = jnp.zeros((8, wide), F32)
            for place, side, r in ((0, 1, 0), (1, 1, 1), (6, 0, 0), (7, 0, 1)):
                tile = jnp.where(wide8 == place, side_ref[side, c, r, pl.ds(z, 1), :], tile)
            first_ref[c, pl.ds(z, 1), rows:, :] = tile[None]
        return carry

    lax.fori_loop(0, layers, border, 0)

    stage_ref[...] = received_ref[...].astype(F32).reshape(stage_ref.shape)
    for c in range(3):
        force_ref[c] = (force_step * unpack(stage_ref, devices, per_owner, tiles, c)).astype(BF16)
    slots_row = table_row(table_ref, devices, per_owner)

    def settle(n):
        load(n).wait()
        placing = one_hot(iota((cells, total), 0) + n * cells == slots_row)
        span = slice(n * chunk, (n + 1) * chunk)
        for c in range(3):
            push = jnp.dot(placing, force_ref[c], preferred_element_type=F32)
            first_ref[c, span, 0:rows, 0:columns] += push.reshape(chunk, rows, columns)

    lane8 = iota((8, wide), 1)
    lane_keep = (lane8 < columns) | (lane8 == columns) & has[3] | (lane8 == wide - 1) & has[2]
    row_keep = (wide8 == 0) & has[1] | (wide8 == 7) & has[0]

    def tile(ref, c, z, t, width):
        return ref[c, z, 8 * t:8 * t + 8, 0:width]

    def neighbours(ref, z, t, width):
        count = tall // 8
        up, down = lax.rem(z + 1, layers), lax.rem(z + layers - 1, layers)
        row = wide8[:, 0:width]
        out = []
        for c in range(3):
            full = tile(ref, c, z, t, wide)
            mid = full[:, 0:width]
            after = tile(ref, c, z, (t + 1) % count, width)
            before = tile(ref, c, z, (t + count - 1) % count, width)
            east = pltpu.roll(jnp.where(row == 0, after, mid), 7, 0)
            west = pltpu.roll(jnp.where(row == 7, before, mid), 1, 0)
            north = pltpu.roll(full, wide - 1, 1)[:, 0:width]
            south = pltpu.roll(full, 1, 1)[:, 0:width]
            out.append((
                mid, east, west, north, south, tile(ref, c, up, t, width),
                tile(ref, c, down, t, width)))
        return [list(v) for v in zip(*out)]

    def step_one(z, carry):
        for t in range(tall // 8):
            new = sweep(*neighbours(first_ref, z, t, wide))
            keep = lane_keep if t < rows // 8 else lane_keep & row_keep
            for c in range(3):
                second_ref[c, z, 8 * t:8 * t + 8, :] = jnp.where(keep, new[c], 0.0)
        return carry

    settle(0)
    settle(1)
    for n in range(2, chunks):
        settle(n)
        lax.fori_loop((n - 1) * chunk, n * chunk, step_one, 0)
    lax.fori_loop(layers - chunk, layers + chunk, lambda z, v: step_one(lax.rem(z, layers), v), 0)

    def step_two(z, carry):
        for t in range(rows // 8):
            new = sweep(*neighbours(second_ref, z, t, columns))
            for c in range(3):
                last_ref[c, z, 8 * t:8 * t + 8, :] = new[c]
        return carry

    def store(n):
        span = pl.ds(n * chunk, chunk)
        return pltpu.make_async_copy(
            last_ref.at[:, span], fluid_ref.at[:, span], out_sem.at[n])

    slots = table_column(table_ref, per_owner)
    for n in range(chunks):
        lax.fori_loop(n * chunk, (n + 1) * chunk, step_two, 0)
        store(n).start()
        taking = one_hot(iota((total, cells), 1) + n * cells == slots)
        for c in range(3):
            flat = last_ref[c, n * chunk:(n + 1) * chunk].reshape(cells, columns).astype(BF16)
            part = jnp.dot(taking, flat, preferred_element_type=F32)
            sum_ref[c] = part if n == 0 else sum_ref[c] + part
    width = 3 * tiles * per_owner
    for c in range(3):
        for p in range(per_owner):
            for t in range(tiles):
                stage_ref[pl.ds(p * 3 * tiles + c * tiles + t, devices, stride=width), :] = (
                    sum_ref[c, p * devices:(p + 1) * devices, t * LANES:(t + 1) * LANES]
                )
    replies_ref[...] = stage_ref[...].reshape(replies_ref.shape).astype(BF16)
    for n in range(chunks):
        store(n).wait()


def gather_kernel(
    rows_grid, columns_grid, per_owner, replies_ref, owners_ref, weights_ref,
    out_ref, returned_ref, loaded_ref, stage_ref, picked_ref, send_sem, recv_sem, own_sem, load_sem,
):
    devices = rows_grid * columns_grid
    blocks, k, points, patch = weights_ref.shape
    tiles = patch // LANES
    total = devices * per_owner

    def load(b):
        return pltpu.make_async_copy(weights_ref.at[b], loaded_ref.at[b], load_sem.at[b])

    for b in range(blocks):
        load(b).start()
    wait = start_swap(
        rows_grid, columns_grid, [replies_ref], [returned_ref], send_sem, recv_sem, own_sem)
    owner_row = to_row(owners_ref[:, 0, :])
    places = slot_column(owner_row, to_column(owner_row), devices)
    selector = one_hot(iota((places.shape[0], total), 1) == places)
    for b in range(blocks):
        load(b).wait()
    wait()
    stage_ref[...] = returned_ref[...].astype(F32).reshape(stage_ref.shape)
    for c in range(3):
        replies = unpack(stage_ref, devices, per_owner, tiles, c).astype(BF16)
        picked_ref[c] = jnp.dot(selector, replies, preferred_element_type=F32)
    diagonal = iota((k, k * points), 0) == iota((k, k * points), 1) // points
    for b in range(blocks):
        rows = [picked_ref[c, b * k:(b + 1) * k, :] for c in range(3)]
        rows.append(jnp.zeros_like(rows[0]))
        left = jnp.concatenate(rows, axis=0).astype(BF16)
        right = loaded_ref[b].reshape(k * points, patch)
        result = lax.dot_general(
            left, right, (((1,), (1,)), ((), ())), preferred_element_type=F32)
        for c in range(3):
            own = jnp.where(diagonal, result[c * k:(c + 1) * k], 0.0)
            fold = own[:, 0:points]
            for n in range(1, k):
                fold = fold + own[:, n * points:(n + 1) * points]
            interp = jnp.sum(fold, axis=0, keepdims=True)
            out_ref[c, b:b + 1, :] = interp


def shards(rows_grid, columns_grid, velocity, fiber_points, stiffness, links, delta_weights,
           owners, patch_slots):
    blocks, intersection, points, patch = delta_weights.shape
    _, layers, rows, columns = velocity.shape
    devices = rows_grid * columns_grid
    entries = blocks * intersection
    per_owner = max(2, (2 * entries + devices - 1) // devices)
    total = devices * per_owner
    tiles = patch // LANES
    width = 3 * tiles * per_owner
    owners = jnp.transpose(owners, (0, 2, 1))
    points_first = jnp.transpose(fiber_points, (1, 0, 2))
    message = jax.ShapeDtypeStruct((devices, width, LANES), BF16)
    table_shape = jax.ShapeDtypeStruct((devices, 1, LANES), I32)
    stage = pltpu.VMEM((devices * width, LANES), F32)
    sides_shape = (2, 3, 2, layers, columns)
    ends_shape = (2, 8, layers * rows)
    received, slots, sides, ends, corners = pl.pallas_call(
        functools.partial(dispatch_kernel, rows_grid, columns_grid, per_owner),
        out_shape=[
            message, table_shape,
            jax.ShapeDtypeStruct(sides_shape, BF16),
            jax.ShapeDtypeStruct(ends_shape, BF16),
            jax.ShapeDtypeStruct((4, 8, LANES), BF16),
        ],
        in_specs=[VMEM, SMEM, VMEM, VMEM, VMEM, ANY, ANY],
        out_specs=[VMEM] * 5,
        scratch_shapes=[
            pltpu.VMEM(message.shape, BF16),
            pltpu.VMEM(table_shape.shape, I32),
            pltpu.VMEM(delta_weights.shape, BF16),
            pltpu.VMEM((3, entries, patch), F32),
            pltpu.VMEM((2, 3, layers, 8, columns), F32),
            pltpu.VMEM((2, 3, layers, rows, LANES), F32),
            pltpu.VMEM((layers * rows, LANES), BF16),
            pltpu.VMEM(ends_shape, F32),
            stage,
            pltpu.VMEM((3, total, patch), BF16),
            pltpu.VMEM(sides_shape, BF16),
            pltpu.VMEM(ends_shape, BF16),
            pltpu.VMEM((2, 8, LANES), BF16),
            *swap_sems(2, devices),
            pltpu.SemaphoreType.DMA((4,)),
            pltpu.SemaphoreType.DMA((blocks,)),
            pltpu.SemaphoreType.DMA((8,)),
            pltpu.SemaphoreType.DMA((8,)),
        ],
        compiler_params=pltpu.CompilerParams(collective_id=0, has_side_effects=True),
    )(points_first, stiffness, links, owners, patch_slots, delta_weights, velocity)

    chunk = 8
    extended = (3, layers, rows + 8, columns + LANES)
    fluid, replies = pl.pallas_call(
        functools.partial(sweeps_kernel, devices, per_owner, rows_grid, columns_grid, chunk),
        out_shape=[jax.ShapeDtypeStruct(velocity.shape, F32), message],
        in_specs=[VMEM] * 5 + [ANY],
        out_specs=[ANY, VMEM],
        scratch_shapes=[
            pltpu.VMEM(extended, F32), pltpu.VMEM(extended, F32), pltpu.VMEM(velocity.shape, F32),
            pltpu.VMEM((2, 3, 2, layers, columns + LANES), F32), stage,
            pltpu.VMEM((3, total, patch), F32), pltpu.VMEM((3, total, patch), BF16),
            pltpu.SemaphoreType.DMA((layers // chunk,)),
            pltpu.SemaphoreType.DMA((layers // chunk,)),
        ],
    )(sides, ends, corners, slots, received, velocity)

    interp = pl.pallas_call(
        functools.partial(gather_kernel, rows_grid, columns_grid, per_owner),
        out_shape=jax.ShapeDtypeStruct(points_first.shape, F32),
        in_specs=[VMEM, VMEM, ANY],
        out_specs=VMEM,
        scratch_shapes=[
            pltpu.VMEM(message.shape, BF16), pltpu.VMEM(delta_weights.shape, BF16), stage,
            pltpu.VMEM((3, entries, patch), F32), *swap_sems(1, devices),
            pltpu.SemaphoreType.DMA((blocks,)),
        ],
        compiler_params=pltpu.CompilerParams(collective_id=1, has_side_effects=True),
    )(replies, owners, delta_weights)
    return fluid, fiber_points + fiber_step * jnp.transpose(interp, (1, 0, 2))


def solution(mesh):
    placed = (
        P(None, None, "gx", "gy"),
        P(("gx", "gy"), None, None),
        P(("gx", "gy")),
        P(("gx", "gy"), None),
        P(("gx", "gy"), None, None, None),
        P(("gx", "gy"), None, None),
        P(("gx", "gy"), None),
    )
    return jax.shard_map(
        functools.partial(shards, mesh.shape["gx"], mesh.shape["gy"]),
        mesh=mesh,
        in_specs=placed,
        out_specs=(placed[0], placed[1]),
        check_vma=False,
    )
```

```python
import functools

import jax
import jax.numpy as jnp
from jax import lax
from jax.experimental import pallas as pl
from jax.experimental.pallas import tpu as pltpu
from jax.sharding import PartitionSpec as P

STEPS = 2
viscosity = 0.1
transport_rate = 0.1
force_step = 0.5
fiber_step = 0.25

F32 = jnp.float32
BF16 = jnp.bfloat16
I32 = jnp.int32
LANES = 128
MESH = pl.DeviceIdType.MESH
VMEM = pl.BlockSpec(memory_space=pltpu.VMEM)
ANY = pl.BlockSpec(memory_space=pl.ANY)
SMEM = pl.BlockSpec(memory_space=pltpu.SMEM)


def iota(shape, dim):
    return lax.broadcasted_iota(I32, shape, dim)


def to_column(row):
    n = row.shape[1]
    return jnp.sum(jnp.where(iota((n, n), 0) == iota((n, n), 1), row, 0), axis=1, keepdims=True)


def to_row(grid):
    n, k = grid.shape
    tiled = jnp.concatenate([grid] * n, axis=1)
    return jnp.sum(
        jnp.where(iota((n, n * k), 0) == iota((n, n * k), 1) // k, tiled, 0), axis=0, keepdims=True)


def slot_row(owner_row, owner_column, devices):
    n = owner_row.shape[1]
    same = (owner_column == owner_row) & (iota((n, n), 0) < iota((n, n), 1))
    rank = jnp.sum(jnp.where(same, 1, 0), axis=0, keepdims=True)
    return rank * devices + owner_row


def slot_column(owner_row, owner_column, devices):
    n = owner_row.shape[1]
    same = (owner_column == owner_row) & (iota((n, n), 1) < iota((n, n), 0))
    rank = jnp.sum(jnp.where(same, 1, 0), axis=1, keepdims=True)
    return rank * devices + owner_column


def spread(
    devices, per_owner, points_ref, stiffness_ref, links_ref, owners_ref, slots_ref, loaded_ref,
    out_ref, table_ref, contrib_ref, stage_ref, wait_block,
):
    blocks, k, points, patch = loaded_ref.shape
    parts = []
    for c in range(3):
        rest = points_ref[c]
        for _ in range(3):
            part = rest.astype(BF16).astype(F32)
            parts.append(part)
            rest = rest - part
    parts.append(jnp.zeros_like(parts[0]))
    parts = jnp.concatenate(parts, axis=0).astype(BF16)
    partner = lax.rem(iota(links_ref.shape, 1) + links_ref[...], points)
    diagonal = iota((k, k * points), 0) == iota((k, k * points), 1) // points
    lefts = []
    for b in range(blocks):
        moving = one_hot(iota((points, points), 0) == partner[b:b + 1])
        there = jnp.dot(parts, moving, preferred_element_type=F32)
        rows = []
        for c in range(3):
            r = 3 * c * blocks + b
            found = there[r:r + 1] + there[r + blocks:r + blocks + 1]
            found = found + there[r + 2 * blocks:r + 2 * blocks + 1]
            row = stiffness_ref[b] * (found - points_ref[c, b:b + 1, :])
            rows.append(jnp.where(diagonal, jnp.concatenate([row] * k, axis=1), 0.0))
        rows.append(jnp.zeros_like(rows[0]))
        lefts.append(jnp.concatenate(rows, axis=0).astype(BF16))

    owner_row = to_row(owners_ref[:, 0, :])
    places = slot_row(owner_row, to_column(owner_row), devices)
    total = devices * per_owner
    chosen = iota((total, places.shape[1]), 0) == places
    selector = one_hot(chosen)

    for b in range(blocks):
        wait_block(b)
        right = loaded_ref[b].reshape(k * points, patch)
        result = jnp.dot(lefts[b], right, preferred_element_type=F32)
        for c in range(3):
            contrib_ref[c, b * k:(b + 1) * k, :] = result[c * k:(c + 1) * k]

    tiles = patch // LANES
    width = 3 * tiles * per_owner
    for c in range(3):
        packed = jnp.dot(selector, contrib_ref[c].astype(BF16), preferred_element_type=F32)
        for p in range(per_owner):
            for t in range(tiles):
                stage_ref[pl.ds(p * 3 * tiles + c * tiles + t, devices, stride=width), :] = (
                    packed[p * devices:(p + 1) * devices, t * LANES:(t + 1) * LANES]
                )
    out_ref[...] = stage_ref[...].reshape(out_ref.shape).astype(BF16)
    column = jnp.max(jnp.where(chosen, to_row(slots_ref[...]), -1), axis=1, keepdims=True)
    lane = iota((devices, LANES), 1)
    table = jnp.full((devices, LANES), -1, I32)
    for p in range(per_owner):
        table = jnp.where(lane == p, column[p * devices:(p + 1) * devices], table)
    for d in range(devices):
        table_ref[d] = table[d:d + 1]


def start_swap(rows, columns, ins, outs, send_sem, recv_sem, own_sem, prepare=None):
    devices = rows * columns
    count = len(ins)
    me = lax.axis_index("gx") * columns + lax.axis_index("gy")

    def place(d):
        return (d // columns, lax.rem(d, columns))

    barrier = pltpu.get_barrier_semaphore()

    def hello(off, carry):
        other = lax.rem(me + off, devices)
        pl.semaphore_signal(barrier, inc=1, device_id=place(other), device_id_type=MESH)
        return carry

    lax.fori_loop(1, devices, hello, 0)
    if prepare is not None:
        prepare()
    pl.semaphore_wait(barrier, devices - 1)

    def copy(n, off):
        other = lax.rem(me + off, devices)
        return pltpu.make_async_remote_copy(
            src_ref=ins[n].at[other], dst_ref=outs[n].at[me],
            send_sem=send_sem.at[n, off], recv_sem=recv_sem.at[n, off],
            device_id=place(other), device_id_type=MESH,
        )

    def start(off, carry):
        for n in range(count):
            copy(n, off).start()
        return carry

    def finish(off, carry):
        for n in range(count):
            copy(n, off).wait()
        return carry

    def own(n):
        return pltpu.make_async_copy(ins[n].at[me], outs[n].at[me], own_sem.at[n])

    lax.fori_loop(1, devices, start, 0)
    for n in range(count):
        own(n).start()

    def wait():
        for n in range(count):
            own(n).wait()
        lax.fori_loop(1, devices, finish, 0)

    return wait


def swap_sems(count, devices):
    return [
        pltpu.SemaphoreType.DMA((count, devices)),
        pltpu.SemaphoreType.DMA((count, devices)),
        pltpu.SemaphoreType.DMA((count,)),
    ]


def unpack(stage_ref, devices, per_owner, tiles, c):
    width = 3 * tiles * per_owner
    rows = []
    for p in range(per_owner):
        rows.append(jnp.concatenate(
            [stage_ref[pl.ds(p * 3 * tiles + c * tiles + t, devices, stride=width), :]
             for t in range(tiles)], axis=1))
    return jnp.concatenate(rows, axis=0)


def table_row(table_ref, devices, per_owner):
    total = devices * per_owner
    row = jnp.zeros((1, total), I32)
    for p in range(per_owner):
        column = table_ref[:, 0, :][:, p:p + 1]
        spot = iota((devices, total), 1) == p * devices + iota((devices, total), 0)
        row = row + jnp.sum(jnp.where(spot, column, 0), axis=0, keepdims=True)
    return row


def table_column(table_ref, per_owner):
    return jnp.concatenate([table_ref[:, 0, :][:, p:p + 1] for p in range(per_owner)], axis=0)


def one_hot(mask):
    return mask.astype(F32).astype(BF16)


def dispatch_kernel(
    rows_grid, columns_grid, per_owner, points_ref, stiffness_ref, links_ref, owners_ref,
    slots_ref, weights_ref, velocity_ref,
    received_ref, table_ref, sides_out, ends_out, corners_out,
    out_ref, outtable_ref, loaded_ref, contrib_ref,
    row_ref, end_ref, edge_ref, ends_ref, stage_ref, force_ref, sides_send, ends_send,
    corners_send, send_sem, recv_sem, own_sem, load_sem, block_sem, hsend_sem, hrecv_sem,
):
    devices = rows_grid * columns_grid
    total = devices * per_owner
    _, layers, rows, columns = velocity_ref.shape
    tiles = columns // LANES
    cells = layers * rows
    loads = []
    for side in range(2):
        loads.append(pltpu.make_async_copy(
            velocity_ref.at[:, :, pl.ds(side * (rows - 8), 8), :], row_ref.at[side],
            load_sem.at[side]))
        loads.append(pltpu.make_async_copy(
            velocity_ref.at[:, :, :, pl.ds(side * (columns - LANES), LANES)], end_ref.at[side],
            load_sem.at[2 + side]))

    def block(b):
        return pltpu.make_async_copy(weights_ref.at[b], loaded_ref.at[b], block_sem.at[b])

    for b in range(weights_ref.shape[0]):
        block(b).start()
    for load in loads:
        load.start()

    def prepare():
        spread(
            devices, per_owner, points_ref, stiffness_ref, links_ref, owners_ref, slots_ref,
            loaded_ref, out_ref, outtable_ref, contrib_ref, stage_ref,
            lambda b: block(b).wait())

    wait = start_swap(
        rows_grid, columns_grid, [out_ref, outtable_ref], [received_ref, table_ref],
        send_sem, recv_sem, own_sem, prepare)

    cell, want = iota((cells, LANES), 0), iota((cells, LANES), 1)
    z, x = cell // rows, lax.rem(cell, rows)
    edge_ref[...] = one_hot((x == 0) & (want == z) | (x == rows - 1) & (want == layers + z))
    r8, l8 = iota((8, LANES), 0), iota((8, LANES), 1)

    def pick(side, c):
        r = r8 - 2 * c
        return one_hot((r >= 0) & (r < 2) & (l8 == r + side * (LANES - 2)))

    for load in loads:
        load.wait()
    across = (((1,), (1,)), ((), ()))
    for side in range(2):
        found = jnp.zeros((8, cells), F32)
        for c in range(3):
            flat = end_ref[side, c].reshape(cells, LANES)
            high = flat.astype(BF16)
            low = (flat - high.astype(F32)).astype(BF16)
            for part in (high, low):
                found = found + lax.dot_general(
                    pick(side, c), part, across, preferred_element_type=F32)
        ends_ref[side] = found

    wait()

    stage_ref[...] = received_ref[...].astype(F32).reshape(stage_ref.shape)
    slots_row = table_row(table_ref, devices, per_owner)
    slots_column = table_column(table_ref, per_owner)
    e = iota((4 * layers, total), 0)
    line, z = e // layers, lax.rem(e, layers)
    x = jnp.where(line < 2, line, rows - 4 + line)
    placing = one_hot(z * rows + x == slots_row)
    for c in range(3):
        force = unpack(stage_ref, devices, per_owner, tiles, c).astype(BF16)
        force_ref[c] = force
        push = jnp.dot(placing, force, preferred_element_type=F32)
        for side in range(2):
            for r in range(2):
                n = side * 2 + r
                v = row_ref[side, c, :, 6 * side + r, :]
                v = v + force_step * push[n * layers:(n + 1) * layers]
                sides_send[side, c, r] = v.astype(BF16)

    gx, gy = lax.axis_index("gx"), lax.axis_index("gy")
    west, east, south, north = gx > 0, gx < rows_grid - 1, gy > 0, gy < columns_grid - 1
    plan = [
        (sides_send.at[0], sides_out.at[1], (-1, 0), west, east),
        (sides_send.at[1], sides_out.at[0], (1, 0), east, west),
        (ends_send.at[0], ends_out.at[1], (0, -1), south, north),
        (ends_send.at[1], ends_out.at[0], (0, 1), north, south),
        (corners_send.at[0], corners_out.at[3], (-1, -1), west & south, east & north),
        (corners_send.at[1], corners_out.at[2], (-1, 1), west & north, east & south),
        (corners_send.at[0], corners_out.at[1], (1, -1), east & south, west & north),
        (corners_send.at[1], corners_out.at[0], (1, 1), east & north, west & south),
    ]
    copies = []
    for n, (source, target, (dx, dy), _, _) in enumerate(plan):
        to = (lax.rem(gx + dx + rows_grid, rows_grid), lax.rem(gy + dy + columns_grid, columns_grid))
        copies.append(pltpu.make_async_remote_copy(
            src_ref=source, dst_ref=target, send_sem=hsend_sem.at[n], recv_sem=hrecv_sem.at[n],
            device_id=to, device_id_type=MESH))

    def go(n):
        @pl.when(plan[n][3])
        def _():
            copies[n].start()

    go(0)
    go(1)
    taking = one_hot(iota((total, cells), 1) == slots_column)
    for side in range(2):
        first = side * (columns - LANES)
        mine = jnp.zeros((8, total), F32)
        for c in range(3):
            mine = mine + lax.dot_general(
                pick(side, c), force_ref[c, :, first:first + LANES], across,
                preferred_element_type=F32)
        push = jnp.dot(mine.astype(BF16), taking, preferred_element_type=F32)
        ends = (ends_ref[side] + force_step * push).astype(BF16)
        ends_send[side] = ends
        corners_send[side] = jnp.dot(
            ends, edge_ref[...], preferred_element_type=F32).astype(BF16)
    for n in range(2, 8):
        go(n)
    for n in range(8):
        @pl.when(plan[n][3])
        def _():
            copies[n].wait_send()

        @pl.when(plan[n][4])
        def _():
            copies[n].wait_recv()


def sweep(mid, east, west, north, south, above, below):
    r = transport_rate
    coefficients = [(viscosity - r * m, viscosity + r * m) for m in mid]
    keep = 1.0 - 6.0 * viscosity
    out = []
    for c in range(3):
        v = keep * mid[c]
        for (ahead, behind), (front, back) in zip(
            coefficients, ((east, west), (north, south), (above, below))
        ):
            v = v + (ahead * front[c] + behind * back[c])
        out.append(v)
    return out


def sweeps_kernel(
    devices, per_owner, rows_grid, columns_grid, chunk, sides_ref, ends_ref, corners_ref,
    table_ref, received_ref, velocity_ref,
    fluid_ref, sum_ref, first_ref, second_ref, last_ref, side_ref, stage_ref,
    force_ref, in_sem, out_sem,
):
    _, layers, rows, columns = velocity_ref.shape
    tiles = columns // LANES
    total = devices * per_owner
    chunks = layers // chunk
    cells = chunk * rows
    tall, wide = rows + 8, columns + LANES

    def load(n):
        span = pl.ds(n * chunk, chunk)
        return pltpu.make_async_copy(
            velocity_ref.at[:, span], first_ref.at[:, span, 0:rows, 0:columns], in_sem.at[n])

    for n in range(chunks):
        load(n).start()

    gx, gy = lax.axis_index("gx"), lax.axis_index("gy")
    has = [gx > 0, gx < rows_grid - 1, gy > 0, gy < columns_grid - 1]
    for side in range(2):
        side_ref[side, :, :, :, 0:columns] = jnp.where(has[side], sides_ref[side].astype(F32), 0.0)
        side_ref[side, :, :, :, columns:] = jnp.zeros((3, 2, layers, LANES), F32)
    r8, l8 = iota((8, LANES), 0), iota((8, LANES), 1)

    def expand(ref, n, side, c, there):
        r = r8 - 2 * c
        pick = one_hot((r >= 0) & (r < 2) & (l8 == r + (1 - side) * (LANES - 2)))
        values = jnp.where(there, ref[n].astype(F32), 0.0).astype(BF16)
        return lax.dot_general(
            values, pick, (((0,), (0,)), ((), ())), preferred_element_type=F32)

    for c in range(3):
        band = expand(ends_ref, 0, 0, c, has[2]) + expand(ends_ref, 1, 1, c, has[3])
        first_ref[c, :, 0:rows, columns:] = band.reshape(layers, rows, LANES)
        low = expand(corners_ref, 0, 0, c, has[0] & has[2])
        low = low + expand(corners_ref, 1, 1, c, has[0] & has[3])
        high = expand(corners_ref, 2, 0, c, has[1] & has[2])
        high = high + expand(corners_ref, 3, 1, c, has[1] & has[3])
        side_ref[0, c, 1, :, columns:] = low[layers:2 * layers]
        side_ref[1, c, 0, :, columns:] = high[0:layers]

    wide8 = iota((8, wide), 0)

    def border(z, carry):
        for c in range(3):
            tile = jnp.zeros((8, wide), F32)
            for place, side, r in ((0, 1, 0), (1, 1, 1), (6, 0, 0), (7, 0, 1)):
                tile = jnp.where(wide8 == place, side_ref[side, c, r, pl.ds(z, 1), :], tile)
            first_ref[c, pl.ds(z, 1), rows:, :] = tile[None]
        return carry

    lax.fori_loop(0, layers, border, 0)

    stage_ref[...] = received_ref[...].astype(F32).reshape(stage_ref.shape)
    for c in range(3):
        force_ref[c] = (force_step * unpack(stage_ref, devices, per_owner, tiles, c)).astype(BF16)
    slots_row = table_row(table_ref, devices, per_owner)

    def settle(n):
        load(n).wait()
        placing = one_hot(iota((cells, total), 0) + n * cells == slots_row)
        span = slice(n * chunk, (n + 1) * chunk)
        for c in range(3):
            push = jnp.dot(placing, force_ref[c], preferred_element_type=F32)
            first_ref[c, span, 0:rows, 0:columns] += push.reshape(chunk, rows, columns)

    lane8 = iota((8, wide), 1)
    lane_keep = (lane8 < columns) | (lane8 == columns) & has[3] | (lane8 == wide - 1) & has[2]
    row_keep = (wide8 == 0) & has[1] | (wide8 == 7) & has[0]

    def tile(ref, c, z, t, width):
        return ref[c, z, 8 * t:8 * t + 8, 0:width]

    def neighbours(ref, z, t, width):
        count = tall // 8
        up, down = lax.rem(z + 1, layers), lax.rem(z + layers - 1, layers)
        row = wide8[:, 0:width]
        out = []
        for c in range(3):
            full = tile(ref, c, z, t, wide)
            mid = full[:, 0:width]
            after = tile(ref, c, z, (t + 1) % count, width)
            before = tile(ref, c, z, (t + count - 1) % count, width)
            east = pltpu.roll(jnp.where(row == 0, after, mid), 7, 0)
            west = pltpu.roll(jnp.where(row == 7, before, mid), 1, 0)
            north = pltpu.roll(full, wide - 1, 1)[:, 0:width]
            south = pltpu.roll(full, 1, 1)[:, 0:width]
            out.append((
                mid, east, west, north, south, tile(ref, c, up, t, width),
                tile(ref, c, down, t, width)))
        return [list(v) for v in zip(*out)]

    def step_one(z, carry):
        for t in range(tall // 8):
            new = sweep(*neighbours(first_ref, z, t, wide))
            for c in range(3):
                if t < rows // 8:
                    second_ref[c, z, 8 * t:8 * t + 8, 0:columns] = new[c][:, 0:columns]
                    second_ref[c, z, 8 * t:8 * t + 8, columns:] = jnp.where(
                        lane_keep[:, columns:], new[c][:, columns:], 0.0)
                else:
                    second_ref[c, z, 8 * t:8 * t + 8, :] = jnp.where(
                        lane_keep & row_keep, new[c], 0.0)
        return carry

    settle(0)
    settle(1)
    for n in range(2, chunks):
        settle(n)
        lax.fori_loop((n - 1) * chunk, n * chunk, step_one, 0)
    lax.fori_loop(layers - chunk, layers + chunk, lambda z, v: step_one(lax.rem(z, layers), v), 0)

    def step_two(z, carry):
        for t in range(rows // 8):
            new = sweep(*neighbours(second_ref, z, t, columns))
            for c in range(3):
                last_ref[c, z, 8 * t:8 * t + 8, :] = new[c]
        return carry

    def store(n):
        span = pl.ds(n * chunk, chunk)
        return pltpu.make_async_copy(
            last_ref.at[:, span], fluid_ref.at[:, span], out_sem.at[n])

    slots = table_column(table_ref, per_owner)
    for n in range(chunks):
        lax.fori_loop(n * chunk, (n + 1) * chunk, step_two, 0)
        store(n).start()
        taking = one_hot(iota((total, cells), 1) + n * cells == slots)
        for c in range(3):
            flat = last_ref[c, n * chunk:(n + 1) * chunk].reshape(cells, columns).astype(BF16)
            part = jnp.dot(taking, flat, preferred_element_type=F32)
            sum_ref[c] = part if n == 0 else sum_ref[c] + part
    for n in range(chunks):
        store(n).wait()


def gather_kernel(
    rows_grid, columns_grid, per_owner, replies_ref, owners_ref, weights_ref,
    out_ref, packed_ref, returned_ref, loaded_ref, stage_ref, picked_ref, send_sem, recv_sem, own_sem, load_sem,
):
    devices = rows_grid * columns_grid
    blocks, k, points, patch = weights_ref.shape
    tiles = patch // LANES
    total = devices * per_owner

    def load(b):
        return pltpu.make_async_copy(weights_ref.at[b], loaded_ref.at[b], load_sem.at[b])

    for b in range(blocks):
        load(b).start()
    width = 3 * tiles * per_owner

    def prepare():
        for c in range(3):
            for p in range(per_owner):
                for t in range(tiles):
                    stage_ref[pl.ds(p * 3 * tiles + c * tiles + t, devices, stride=width), :] = (
                        replies_ref[c, p * devices:(p + 1) * devices, t * LANES:(t + 1) * LANES]
                    )
        packed_ref[...] = stage_ref[...].reshape(packed_ref.shape).astype(BF16)

    wait = start_swap(
        rows_grid, columns_grid, [packed_ref], [returned_ref], send_sem, recv_sem, own_sem,
        prepare)
    owner_row = to_row(owners_ref[:, 0, :])
    places = slot_column(owner_row, to_column(owner_row), devices)
    selector = one_hot(iota((places.shape[0], total), 1) == places)
    for b in range(blocks):
        load(b).wait()
    wait()
    stage_ref[...] = returned_ref[...].astype(F32).reshape(stage_ref.shape)
    for c in range(3):
        replies = unpack(stage_ref, devices, per_owner, tiles, c).astype(BF16)
        picked_ref[c] = jnp.dot(selector, replies, preferred_element_type=F32)
    diagonal = iota((k, k * points), 0) == iota((k, k * points), 1) // points
    for b in range(blocks):
        rows = [picked_ref[c, b * k:(b + 1) * k, :] for c in range(3)]
        rows.append(jnp.zeros_like(rows[0]))
        left = jnp.concatenate(rows, axis=0).astype(BF16)
        right = loaded_ref[b].reshape(k * points, patch)
        result = lax.dot_general(
            left, right, (((1,), (1,)), ((), ())), preferred_element_type=F32)
        for c in range(3):
            own = jnp.where(diagonal, result[c * k:(c + 1) * k], 0.0)
            fold = own[:, 0:points]
            for n in range(1, k):
                fold = fold + own[:, n * points:(n + 1) * points]
            interp = jnp.sum(fold, axis=0, keepdims=True)
            out_ref[c, b:b + 1, :] = interp


def shards(rows_grid, columns_grid, velocity, fiber_points, stiffness, links, delta_weights,
           owners, patch_slots):
    blocks, intersection, points, patch = delta_weights.shape
    _, layers, rows, columns = velocity.shape
    devices = rows_grid * columns_grid
    entries = blocks * intersection
    per_owner = max(2, (2 * entries + devices - 1) // devices)
    total = devices * per_owner
    tiles = patch // LANES
    width = 3 * tiles * per_owner
    owners = jnp.transpose(owners, (0, 2, 1))
    points_first = jnp.transpose(fiber_points, (1, 0, 2))
    message = jax.ShapeDtypeStruct((devices, width, LANES), BF16)
    table_shape = jax.ShapeDtypeStruct((devices, 1, LANES), I32)
    stage = pltpu.VMEM((devices * width, LANES), F32)
    sides_shape = (2, 3, 2, layers, columns)
    ends_shape = (2, 8, layers * rows)
    received, slots, sides, ends, corners = pl.pallas_call(
        functools.partial(dispatch_kernel, rows_grid, columns_grid, per_owner),
        out_shape=[
            message, table_shape,
            jax.ShapeDtypeStruct(sides_shape, BF16),
            jax.ShapeDtypeStruct(ends_shape, BF16),
            jax.ShapeDtypeStruct((4, 8, LANES), BF16),
        ],
        in_specs=[VMEM, SMEM, VMEM, VMEM, VMEM, ANY, ANY],
        out_specs=[VMEM] * 5,
        scratch_shapes=[
            pltpu.VMEM(message.shape, BF16),
            pltpu.VMEM(table_shape.shape, I32),
            pltpu.VMEM(delta_weights.shape, BF16),
            pltpu.VMEM((3, entries, patch), F32),
            pltpu.VMEM((2, 3, layers, 8, columns), F32),
            pltpu.VMEM((2, 3, layers, rows, LANES), F32),
            pltpu.VMEM((layers * rows, LANES), BF16),
            pltpu.VMEM(ends_shape, F32),
            stage,
            pltpu.VMEM((3, total, patch), BF16),
            pltpu.VMEM(sides_shape, BF16),
            pltpu.VMEM(ends_shape, BF16),
            pltpu.VMEM((2, 8, LANES), BF16),
            *swap_sems(2, devices),
            pltpu.SemaphoreType.DMA((4,)),
            pltpu.SemaphoreType.DMA((blocks,)),
            pltpu.SemaphoreType.DMA((8,)),
            pltpu.SemaphoreType.DMA((8,)),
        ],
        compiler_params=pltpu.CompilerParams(collective_id=0, has_side_effects=True),
    )(points_first, stiffness, links, owners, patch_slots, delta_weights, velocity)

    chunk = 8
    extended = (3, layers, rows + 8, columns + LANES)
    fluid, replies = pl.pallas_call(
        functools.partial(sweeps_kernel, devices, per_owner, rows_grid, columns_grid, chunk),
        out_shape=[
            jax.ShapeDtypeStruct(velocity.shape, F32),
            jax.ShapeDtypeStruct((3, total, patch), F32),
        ],
        in_specs=[VMEM] * 5 + [ANY],
        out_specs=[ANY, VMEM],
        scratch_shapes=[
            pltpu.VMEM(extended, F32), pltpu.VMEM(extended, F32), pltpu.VMEM(velocity.shape, F32),
            pltpu.VMEM((2, 3, 2, layers, columns + LANES), F32), stage,
            pltpu.VMEM((3, total, patch), BF16),
            pltpu.SemaphoreType.DMA((layers // chunk,)),
            pltpu.SemaphoreType.DMA((layers // chunk,)),
        ],
    )(sides, ends, corners, slots, received, velocity)

    interp = pl.pallas_call(
        functools.partial(gather_kernel, rows_grid, columns_grid, per_owner),
        out_shape=jax.ShapeDtypeStruct(points_first.shape, F32),
        in_specs=[VMEM, VMEM, ANY],
        out_specs=VMEM,
        scratch_shapes=[
            pltpu.VMEM(message.shape, BF16), pltpu.VMEM(message.shape, BF16),
            pltpu.VMEM(delta_weights.shape, BF16), stage,
            pltpu.VMEM((3, entries, patch), F32), *swap_sems(1, devices),
            pltpu.SemaphoreType.DMA((blocks,)),
        ],
        compiler_params=pltpu.CompilerParams(collective_id=1, has_side_effects=True),
    )(replies, owners, delta_weights)
    return fluid, fiber_points + fiber_step * jnp.transpose(interp, (1, 0, 2))


def solution(mesh):
    placed = (
        P(None, None, "gx", "gy"),
        P(("gx", "gy"), None, None),
        P(("gx", "gy")),
        P(("gx", "gy"), None),
        P(("gx", "gy"), None, None, None),
        P(("gx", "gy"), None, None),
        P(("gx", "gy"), None),
    )
    return jax.shard_map(
        functools.partial(shards, mesh.shape["gx"], mesh.shape["gy"]),
        mesh=mesh,
        in_specs=placed,
        out_specs=(placed[0], placed[1]),
        check_vma=False,
    )
```
